32 devices in a mesh: group: 2 (over x), expert: 8 (over z, y), tensor: 2 (over core).
Axes of the slice: x: 2, y: 2, z: 4, core: 2. Of those that a mesh axis runs over, the one named last changes fastest.
Arguments:
- tokens: bfloat16 [1024, 3072], P(('group', 'expert'), 'tensor'), parts along dimension 0, may hold values from -6 to 6
- expert_ids: int32 [1024, 2], P(('group', 'expert')), parts along dimension 0, may hold values from 0 to 3, all different within a row; in each aligned block of 64 rows (0 to 63, 64 to 127, ...) at most 48 rows name the same one
- gate_fixed: int32 [1024, 2], P(('group', 'expert')), parts along dimension 0, may hold values from 1 to 65535
- gate_weight: bfloat16 [8, 3072, 4096], P('expert', None, 'tensor'), may hold values from -0.109375 to 0.109375
- up_weight: bfloat16 [8, 3072, 4096], P('expert', None, 'tensor'), may hold values from -0.109375 to 0.109375
- down_weight: bfloat16 [8, 4096, 3072], P('expert', 'tensor'), may hold values from -0.0625 to 0.0625
Outputs:
- mixed_out: bfloat16 [1024, 3072], P(('group', 'expert'), 'tensor'), parts along dimension 0
The draws below stay inside these ranges and needn't reach their ends.
There are 2 independent parts, one for each index of `group`. The reference program is written for one: setup_inputs(seed, part) draws one part's arguments, and reference() takes and returns one part's arrays. A program takes and returns all parts, laid end to end along the dimension named above; an argument that names none is the same for every part. Nothing has to cross between parts.
Inputs may be any that keep to these rules, and one draw needn't show every extreme that they name: `expert_ids`: each token names 2 different experts. Among the tokens of one block of 64, at most 48 name one expert, and in every draw some expert is named by exactly 48 tokens of some block. `gate_fixed`: router weights in units of 1/65536.
All inputs are finite; a program needn't handle non-finite values.
Results may differ from the reference program's by a relative error of at most 0.0058.
Values may be sent and summed in bfloat16 or wider, within the bound.
A program may use at most 128 MiB of HBM per device.

```python
import math
import jax
import jax.numpy as jnp
import numpy as np
from jax import lax

D = 3072
FF = 8192
EXPERTS = 4
TOP = 2
TOK_DEV = 64
CAP = 48
FF_S = 4096
TOKENS = 512
N_EXPERT = 8


def touch_ends(values, key, least, high):
    place = [jax.random.randint(jax.random.fold_in(key, axis), (), 0, length) for axis, length in enumerate(values.shape)]
    main_axis = values.shape.index(max(values.shape))
    neighbour = place[:main_axis] + [(place[main_axis] + 1) % values.shape[main_axis]] + place[main_axis + 1:]
    return values.at[tuple(place)].set(least).at[tuple(neighbour)].set(high)


def steps_of(key, dims, shards, least, high):
    def one(dim, parts):
        draws = jax.random.uniform(jax.random.fold_in(jax.random.fold_in(key, 6), dim), (parts,), jnp.float32, least / len(shards), high / len(shards))
        return jnp.repeat(jnp.exp(draws), dims[dim] // parts).reshape((-1,) + (1,) * (len(dims) - dim - 1))

    gain = one(*shards[0])
    for cut in shards[1:]:
        gain = gain * one(*cut)
    return gain


def routed_block(stream_key, own, number, rows, amount, top, bound, slope):
    order = jax.random.permutation(stream_key, amount)
    heavy_load, common = load_shares(amount, rows * top, bound, slope, True), load_shares(amount, rows * top, bound, slope, False)
    places = jnp.arange(amount)

    def named(lengths, turn):
        used = int((lengths > 0).sum())
        fixed = max(1, used // 4)
        moved = fixed + (places - fixed + turn * (used - fixed)) % max(1, amount - fixed)
        return jnp.zeros((amount,), jnp.int32).at[order[jnp.where(places < fixed, places, moved)]].set(jnp.asarray(lengths, jnp.int32))

    lengths = jnp.where(number % 4 == 0, named(heavy_load, number // 4), named(common, number - number // 4 - 1))
    mixed = jax.random.permutation(jax.random.fold_in(own, 3), amount)
    giver, sink = mixed[0:amount // 2 * 2:2], mixed[1:amount // 2 * 2:2]
    margin = jnp.minimum(lengths[giver] - 1, bound - lengths[sink]) // 2
    margin = jnp.where((giver == order[0]) | (sink == order[0]) | (lengths[sink] == 0), 0, jnp.maximum(margin, 0))
    moved = jax.random.randint(jax.random.fold_in(own, 4), (amount // 2,), 0, 1 << 20) % (margin + 1)
    lengths = lengths.at[giver].add(-moved).at[sink].add(moved)
    members = jnp.searchsorted(jnp.cumsum(lengths), jnp.arange(rows * top), side="right").astype(jnp.int32)
    table = members.reshape(top, rows).T
    table = table[jax.random.permutation(jax.random.fold_in(own, 1), rows)]
    turn = jax.random.randint(jax.random.fold_in(own, 2), (rows, 1), 0, top)
    return jnp.take_along_axis(table, (jnp.arange(top)[None, :] + turn) % top, axis=1)


def load_shares(count, total, most, slope, full):
    loads = [(1 << 20) // math.isqrt(standing ** slope) + 1 for standing in range(1, count + 1)]
    largest = most if full else min(most, max(-(-total // count), total * loads[0] // sum(loads)))
    least = 1 if total - largest >= count - 1 else 0
    given, surplus = [largest] + [least] * (count - 1), total - largest - least * (count - 1)
    while surplus > 0:
        free = [i for i in range(1, count) if given[i] < largest] or [i for i in range(1, count) if given[i] < most]
        pool, left = sum([loads[i] for i in free]), surplus
        for i in free:
            addition = min(most - given[i], max(1, left * loads[i] // pool), surplus)
            given[i] = given[i] + addition
            surplus = surplus - addition
    return np.array(given)


def normal_values(stream_key, extent, deviation, most, cuts=(), kind=jnp.bfloat16):
    result = deviation * jax.random.normal(stream_key, extent, jnp.float32)
    if cuts:
        result = result * steps_of(stream_key, extent, cuts, -0.22, 0.18)
    return jnp.clip(result, -most, most).astype(kind)


def setup_inputs(seed: int = 0, part: int = 0) -> dict:
    keys = jax.random.split(jax.random.key(seed), 7)
    part_splits = jax.random.split(jax.random.fold_in(keys[6], part), 7)
    tokens = normal_values(part_splits[0], (TOKENS, D), 1.0, 6.0, ((0, 8), (1, 2)))
    expert_ids_keys = jax.random.split(jax.random.fold_in(part_splits[1], 1), TOKENS // TOK_DEV)
    expert_ids_turns = jax.random.permutation(jax.random.fold_in(part_splits[1], 3), TOKENS // TOK_DEV)
    expert_ids = jax.vmap(lambda own, number: routed_block(jax.random.fold_in(part_splits[1], 2), own, number, TOK_DEV, EXPERTS, TOP, CAP, 2))(expert_ids_keys, expert_ids_turns).reshape((TOKENS, TOP))
    gate_fixed = touch_ends(jax.random.randint(part_splits[2], (TOKENS, TOP), 1, 65536), jax.random.fold_in(part_splits[2], 1), 1, 65535).astype(jnp.int32)
    gate_weight = normal_values(keys[3], (N_EXPERT, D, FF_S), D ** -0.5, 0.109375, ((0, 8), (2, 2)))
    up_weight = normal_values(keys[4], (N_EXPERT, D, FF_S), D ** -0.5, 0.109375, ((0, 8), (2, 2)))
    down_weight = normal_values(keys[5], (N_EXPERT, FF_S, D), FF ** -0.5, 0.0625, ((0, 8), (1, 2)))
    return dict(tokens=tokens, expert_ids=expert_ids, gate_fixed=gate_fixed, gate_weight=gate_weight, up_weight=up_weight, down_weight=down_weight)


def slot_numbers(expert_ids, block_rows):
    flat_ids = expert_ids.reshape(-1, block_rows * TOP)
    matches = (flat_ids[:, :, None] == jnp.arange(EXPERTS, dtype=jnp.int32)[None, None, :]).astype(jnp.int32)
    before = jnp.cumsum(matches, axis=1) - matches
    return jnp.sum(before * matches, axis=2).reshape(expert_ids.shape).astype(jnp.int32)


def reference(tokens, expert_ids, gate_fixed, gate_weight, up_weight, down_weight):
    slices = N_EXPERT // EXPERTS
    slot_pos = slot_numbers(expert_ids, TOK_DEV)
    fixed_gate = gate_fixed.astype(jnp.float32)
    gate_share = fixed_gate / jnp.sum(fixed_gate, axis=1, keepdims=True)
    block_idx = (jnp.arange(TOKENS, dtype=jnp.int32) // TOK_DEV)[:, None]
    target = ((block_idx * EXPERTS + expert_ids) * CAP + slot_pos).astype(jnp.int32)
    dispatch_rows = jnp.zeros((N_EXPERT * EXPERTS * CAP, D), jnp.bfloat16)
    dispatch_rows = dispatch_rows.at[target.reshape(-1)].set(jnp.repeat(tokens, TOP, axis=0))
    dispatched = dispatch_rows.reshape(N_EXPERT, EXPERTS, CAP, D)

    def one_expert(expert_idx):
        rows_in = lax.dynamic_index_in_dim(dispatched, expert_idx, axis=1, keepdims=False).reshape(N_EXPERT * CAP, D)
        running = jnp.zeros((N_EXPERT * CAP, D), jnp.float32)
        for slice_idx in range(slices):
            owner_idx = expert_idx * slices + slice_idx
            w_gate = lax.dynamic_index_in_dim(gate_weight, owner_idx, 0, keepdims=False)
            w_up = lax.dynamic_index_in_dim(up_weight, owner_idx, 0, keepdims=False)
            w_down = lax.dynamic_index_in_dim(down_weight, owner_idx, 0, keepdims=False)
            gate_vals = jnp.dot(rows_in, w_gate, preferred_element_type=jnp.float32)
            up_vals = jnp.dot(rows_in, w_up, preferred_element_type=jnp.float32)
            hidden = (jax.nn.silu(gate_vals) * up_vals).astype(jnp.bfloat16)
            slice_out = jnp.dot(hidden, w_down, preferred_element_type=jnp.float32).astype(jnp.bfloat16)
            slice_out = lax.optimization_barrier(slice_out)
            running = running + slice_out.astype(jnp.float32)
        return running

    expert_out = lax.map(one_expert, jnp.arange(EXPERTS, dtype=jnp.int32))
    row_index = ((expert_ids * N_EXPERT + block_idx) * CAP + slot_pos).astype(jnp.int32)
    picked = expert_out.reshape(-1, D)[row_index]
    mixed_out = jnp.sum(gate_share[:, :, None] * picked, axis=1)
    return mixed_out.astype(jnp.bfloat16)
```

```python
import functools

import jax
import jax.numpy as jnp
from jax import lax
from jax.experimental import pallas as pl
from jax.experimental.pallas import tpu as pltpu
from jax.sharding import PartitionSpec as P

EXPERTS = 4
TILE = 1024
DOWN_TILE = 768
F32 = jnp.float32
BF16 = jnp.bfloat16


def ring_kernel(n, tok, ids, fixed, wg, wu, wd, out,
           xb, wt, hid, yown, ysend, zin, psend, precv, vg, vu, vd,
           g_sem, u_sem, d_sem, x_ssem, x_rsem, w_ssem, w_rsem, b_ssem, b_rsem,
           z_ssem, z_rsem, p_ssem, p_rsem):
    h = n // 2
    rows, half = tok.shape
    part = rows // 2
    me = lax.axis_index("expert")
    core = lax.axis_index("tensor")
    other = 1 - core
    expert = me // (n // EXPERTS)
    odd = me % 2
    pos = (1 - odd) * (me // 2) + odd * (n - 1 - me // 2)

    def at_pos(p):
        p = (p + n) % n
        back = p // h
        return (1 - back) * (2 * p) + back * (2 * (n - 1 - p) + 1)

    onward = ({"expert": at_pos(pos + 1)}, {"expert": at_pos(pos - 1)})
    sibling = {"tensor": other}

    ff = hid.shape[1]
    tile = min(TILE, ff)
    j_hidden = ff // tile
    j_half = half // DOWN_TILE

    def hidden_cols(j):
        return pl.ds(pl.multiple_of(j * tile, tile), tile)

    def out_cols(j):
        return pl.ds(pl.multiple_of(j * DOWN_TILE, DOWN_TILE), DOWN_TILE)

    def weight_copies(j):
        cols = hidden_cols(j)
        return (pltpu.make_async_copy(wg.at[0, :, cols], vg.at[:, cols], g_sem.at[j]),
                pltpu.make_async_copy(wu.at[0, :, cols], vu.at[:, cols], u_sem.at[j]))

    def down_copy(j):
        cols = out_cols(j)
        return pltpu.make_async_copy(wd.at[0, :, cols], vd.at[:, cols], d_sem.at[j])

    @pl.loop(0, j_hidden)
    def _(j):
        for copy in weight_copies(j):
            copy.start()

    @pl.loop(0, 2 * j_half)
    def _(j):
        down_copy(j).start()

    barrier = pltpu.get_barrier_semaphore()
    for target in onward + (sibling,):
        pl.semaphore_signal(barrier, inc=1, device_id=target, device_id_type=pl.DeviceIdType.MESH)

    diag = (lax.broadcasted_iota(jnp.int32, (rows, 128), 0)
            == lax.broadcasted_iota(jnp.int32, (rows, 128), 1))
    f0 = fixed[:, 0:1].astype(F32)
    f1 = fixed[:, 1:2].astype(F32)
    total = f0 + f1
    s0, s1 = f0 / total, f1 / total
    i0, i1 = ids[:, 0:1], ids[:, 1:2]
    wt[0, 0] = jnp.zeros((8, 128), F32)
    for e in range(EXPERTS):
        col = jnp.where(i0 == e, s0, 0.0) + jnp.where(i1 == e, s1, 0.0)
        wt[0, 0, e:e + 1, :] = jnp.sum(jnp.where(diag, col, 0.0), axis=0, keepdims=True)
    xb[0, core, 0:rows, :] = tok[...]
    pl.semaphore_wait(barrier, 3)

    def remote(src, dst, ssem, rsem, target):
        return pltpu.make_async_remote_copy(
            src_ref=src, dst_ref=dst, send_sem=ssem, recv_sem=rsem,
            device_id=target, device_id_type=pl.DeviceIdType.MESH)

    def x_copy(d, s, q):
        piece = pl.ds(d * rows + q * part, part)
        return remote(xb.at[s - 1, core, piece], xb.at[s, core, piece],
                      x_ssem.at[d, s, q], x_rsem.at[d, s, q], onward[d])

    def x_first(d, q):
        return remote(xb.at[0, core, pl.ds(q * part, part)],
                      xb.at[1, core, pl.ds(d * rows + q * part, part)],
                      x_ssem.at[d, 1, q], x_rsem.at[d, 1, q], onward[d])

    def x_last(d):
        return remote(xb.at[h - 1, core, pl.ds(d * rows + d * part, part)],
                      xb.at[0, core, pl.ds(rows + d * part, part)],
                      x_ssem.at[d, h, d], x_rsem.at[d, h, d], onward[d])

    def w_copy(d, s):
        return remote(wt.at[s - 1, d], wt.at[s, d], w_ssem.at[d, s], w_rsem.at[d, s], onward[d])

    def w_first(d):
        return remote(wt.at[0, 0], wt.at[1, d], w_ssem.at[d, 1], w_rsem.at[d, 1], onward[d])

    def w_last():
        return remote(wt.at[h - 1, 0], wt.at[0, 1], w_ssem.at[0, h], w_rsem.at[0, h], onward[0])

    def b_copy(d, s):
        place = xb.at[s, core, pl.ds(d * rows, rows)]
        return remote(place, place, b_ssem.at[d, s], b_rsem.at[d, s], sibling)

    def z_copy(s):
        return remote(ysend.at[s], zin.at[s], z_ssem.at[s], z_rsem.at[s], sibling)

    for d in range(2):
        w_first(d).start()
    for q in range(2):
        for d in range(2):
            x_first(d, d if q == 0 else 1 - d).start()
    b_copy(0, 0).start()

    def compute(s, first):
        @pl.loop(0, j_hidden)
        def _(j):
            cols = hidden_cols(j)

            @pl.when(first)
            def _():
                for copy in weight_copies(j):
                    copy.wait()

            a, b = xb[s, 0], xb[s, 1]
            g = (jnp.dot(a, vg[0:half, cols], preferred_element_type=F32)
                 + jnp.dot(b, vg[half:2 * half, cols], preferred_element_type=F32))
            u = (jnp.dot(a, vu[0:half, cols], preferred_element_type=F32)
                 + jnp.dot(b, vu[half:2 * half, cols], preferred_element_type=F32))
            hid[:, cols] = (g / (1.0 + jnp.exp(-g)) * u).astype(BF16)

        share = jnp.concatenate(
            [jnp.sum(jnp.where(diag, wt[s, d, pl.ds(expert, 1), :], 0.0), axis=1, keepdims=True)
             for d in range(2)], axis=0)

        def down(j, which):
            cols = pl.ds(pl.multiple_of(which * half + j * DOWN_TILE, DOWN_TILE), DOWN_TILE)

            @pl.when(first)
            def _():
                down_copy(which * j_half + j).wait()

            return jnp.dot(hid[...], vd[:, cols], preferred_element_type=F32) * share

        @pl.loop(0, j_half)
        def _(j):
            ysend[s, :, out_cols(j)] = down(j, other).astype(BF16)

        z_copy(s).start()

        @pl.loop(0, j_half)
        def _(j):
            yown[s, :, out_cols(j)] = down(j, core)

    def step(s, carry):
        for turn in range(2):
            for d in range(2):
                q = d if turn == 0 else 1 - d
                x_copy(d, s, q).wait_recv()

                @pl.when(s < h - 1)
                def _():
                    x_copy(d, s + 1, q).start()

                if turn == 0:
                    @pl.when(s == h - 1)
                    def _():
                        x_last(d).start()

        for d in range(2):
            w_copy(d, s).wait_recv()

        @pl.when(s < h - 1)
        def _():
            for d in range(2):
                w_copy(d, s + 1).start()

        @pl.when(s == h - 1)
        def _():
            w_last().start()

        for d in range(2):
            b_copy(d, s).start()
        for d in range(2):
            b_copy(d, s).wait_recv()
        compute(s, s == 1)
        return carry

    lax.fori_loop(1, h, step, 0)
    for d in range(2):
        x_last(d).wait_recv()
    w_last().wait_recv()
    b_copy(1, 0).start()
    b_copy(0, 0).wait_recv()
    b_copy(1, 0).wait_recv()
    compute(0, False)

    def p_copy(d, k, q):
        piece = pl.ds(q * part, part)
        return remote(psend.at[d, k, piece], precv.at[d, k, piece],
                      p_ssem.at[d, k, q], p_rsem.at[d, k, q], onward[d])

    z_copy(0).wait_recv()
    for k in range(h, 0, -1):
        slot = k % h
        if k < h:
            z_copy(k).wait_recv()
        for turn in range(2):
            for d in range(2):
                q = (1 - d) if turn == 0 else d
                if k == h and q != d:
                    continue
                base = (rows if k == h or d == 0 else 0) + q * part
                total = yown[slot, base:base + part, :] + zin[slot, base:base + part, :].astype(F32)
                if k < h - 1 or (k == h - 1 and q == d):
                    p_copy(d, k, q).wait_recv()
                    total = total + precv[d, k, q * part:(q + 1) * part, :].astype(F32)
                psend[d, k - 1, q * part:(q + 1) * part, :] = total.astype(BF16)
                p_copy(d, k - 1, q).start()
    for q in (0, 1):
        total = yown[0, q * part:(q + 1) * part, :] + zin[0, q * part:(q + 1) * part, :].astype(F32)
        for d in range(2):
            p_copy(d, 0, q).wait_recv()
            total = total + precv[d, 0, q * part:(q + 1) * part, :].astype(F32)
        out[q * part:(q + 1) * part, :] = total.astype(BF16)

    for d in range(2):
        for q in range(2):
            x_first(d, q).wait_send()
        w_first(d).wait_send()
        x_last(d).wait_send()
        for k in range(h):
            for q in range(2):
                if k < h - 1 or q == d:
                    p_copy(d, k, q).wait_send()
    w_last().wait_send()

    def drain(s, carry):
        for d in range(2):
            for q in range(2):
                x_copy(d, s, q).wait_send()
            w_copy(d, s).wait_send()
        return carry

    lax.fori_loop(2, h, drain, 0)

    def drain_sibling(s, carry):
        for d in range(2):
            b_copy(d, s).wait_send()
        z_copy(s).wait_send()
        return carry

    lax.fori_loop(0, h, drain_sibling, 0)


def ring_per_device(tokens, expert_ids, gate_fixed, gate_weight, up_weight, down_weight):
    n = lax.axis_size("expert")
    h = n // 2
    rows, half = tokens.shape
    ff = gate_weight.shape[2]
    dma = pltpu.SemaphoreType.DMA
    vmem = pl.BlockSpec(memory_space=pltpu.VMEM)
    hbm = pl.BlockSpec(memory_space=pl.ANY)
    return pl.pallas_call(
        functools.partial(ring_kernel, n),
        out_shape=jax.ShapeDtypeStruct((rows, half), BF16),
        in_specs=[vmem, vmem, vmem, hbm, hbm, hbm],
        out_specs=vmem,
        scratch_shapes=[
            pltpu.VMEM((h, 2, 2 * rows, half), BF16),
            pltpu.VMEM((h, 2, 8, 128), F32),
            pltpu.VMEM((2 * rows, ff), BF16),
            pltpu.VMEM((h, 2 * rows, half), F32),
            pltpu.VMEM((h, 2 * rows, half), BF16),
            pltpu.VMEM((h, 2 * rows, half), BF16),
            pltpu.VMEM((2, h, rows, half), BF16),
            pltpu.VMEM((2, h, rows, half), BF16),
            pltpu.VMEM((2 * half, ff), BF16),
            pltpu.VMEM((2 * half, ff), BF16),
            pltpu.VMEM((ff, 2 * half), BF16),
            dma((ff // min(TILE, ff),)), dma((ff // min(TILE, ff),)), dma((2 * half // DOWN_TILE,)),
            dma((2, h + 1, 2)), dma((2, h + 1, 2)),
            dma((2, h + 1)), dma((2, h + 1)),
            dma((2, h)), dma((2, h)),
            dma((h,)), dma((h,)),
            dma((2, h, 2)), dma((2, h, 2)),
        ],
        compiler_params=pltpu.CompilerParams(
            collective_id=0, has_side_effects=True, vmem_limit_bytes=60 * 1024 * 1024),
    )(tokens, expert_ids, gate_fixed, gate_weight, up_weight, down_weight)


CAP = 48
CHUNK = 16
PARTS = CAP // CHUNK
GU_TILE = 1024


def slot_kernel(tok, ids, fixed, wg, wu, wd, out,
                pk, xb, hid, yown, ysend, zin, psend, precv, rsend, ret, pick, vg, vu, vd,
                g_sem, u_sem, d_sem, z_ssem, z_rsem, y_ssem, y_rsem, b_ssem, b_rsem,
                k_ssem, k_rsem, p_ssem, p_rsem, r_ssem, r_rsem):
    rows, half = tok.shape
    ff = hid.shape[1]
    block = EXPERTS * CHUNK
    me = lax.axis_index("expert")
    core = lax.axis_index("tensor")
    other = 1 - core
    z, y = me // 2, me % 2

    def flip(r):
        hi = z // 2 if r < 2 else 1 - z // 2
        lo = z % 2 if r % 2 == 0 else 1 - z % 2
        return 2 * hi + lo

    sibling = {"tensor": other}
    across = {"expert": 2 * z + 1 - y}
    along = {r: {"expert": 2 * flip(r) + y} for r in range(1, EXPERTS)}

    barrier = pltpu.get_barrier_semaphore()
    for target in (*along.values(), across, sibling):
        pl.semaphore_signal(barrier, inc=1, device_id=target, device_id_type=pl.DeviceIdType.MESH)

    tile = min(GU_TILE, ff)
    tiles = ff // tile

    def weight_copies(j):
        cols = pl.ds(j * tile, tile)
        return (pltpu.make_async_copy(wg.at[0, :, cols], vg.at[:, cols], g_sem.at[j]),
                pltpu.make_async_copy(wu.at[0, :, cols], vu.at[:, cols], u_sem.at[j]))

    def down_copy(which):
        cols = pl.ds(pl.multiple_of(which * half, half), half)
        return pltpu.make_async_copy(wd.at[0, :, cols], vd.at[:, cols], d_sem.at[which])

    for j in range(tiles):
        for copy in weight_copies(j):
            copy.start()
    down_copy(other).start()
    down_copy(core).start()

    i0, i1 = ids[0:1, :], ids[1:2, :]
    match = [jnp.where((i0 == flip(r)) | (i1 == flip(r)), 1.0, 0.0) for r in range(EXPERTS)]
    before = (lax.broadcasted_iota(jnp.int32, (rows, rows), 0)
              < lax.broadcasted_iota(jnp.int32, (rows, rows), 1))
    stacked = jnp.concatenate(match + [jnp.zeros((8 - EXPERTS, rows), F32)], axis=0)
    pos = jnp.dot(stacked.astype(BF16), jnp.where(before, 1.0, 0.0).astype(BF16),
                  preferred_element_type=F32)
    slot = [jnp.where(match[r] > 0.0, pos[r:r + 1, :], -1.0) for r in range(EXPERTS)]
    number = lax.broadcasted_iota(jnp.int32, (CAP, rows), 0).astype(F32)
    for r in range(EXPERTS):
        chosen = jnp.where(slot[r] == number, 1.0, 0.0).astype(BF16)
        pk[r] = jnp.dot(chosen, tok[...], preferred_element_type=F32).astype(BF16)
    pl.semaphore_wait(barrier, EXPERTS + 1)

    def remote(src, dst, ssem, rsem, target):
        return pltpu.make_async_remote_copy(
            src_ref=src, dst_ref=dst, send_sem=ssem, recv_sem=rsem,
            device_id=target, device_id_type=pl.DeviceIdType.MESH)

    def slots(c):
        return pl.ds(pl.multiple_of(c * CHUNK, CHUNK), CHUNK)

    def unit(q, r):
        return pl.ds(q * block + r * CHUNK, CHUNK)

    def z_copy(r, c):
        return remote(pk.at[r, slots(c)], xb.at[c, core, unit(0, r)],
                      z_ssem.at[r, c], z_rsem.at[r, c], along[r])

    def y_copy(r, c):
        src = pk.at[0, slots(c)] if r == 0 else xb.at[c, core, unit(0, r)]
        return remote(src, xb.at[c, core, unit(1, r)], y_ssem.at[r, c], y_rsem.at[r, c], across)

    def b_copy(q, c):
        place = xb.at[c, core, pl.ds(q * block, block)]
        return remote(place, place, b_ssem.at[q, c], b_rsem.at[q, c], sibling)

    def k_copy(c):
        return remote(ysend.at[c], zin.at[c], k_ssem.at[c], k_rsem.at[c], sibling)

    def p_copy(r, c):
        return remote(psend.at[c, unit(0, r)], precv.at[c, unit(0, r)],
                      p_ssem.at[r, c], p_rsem.at[r, c], across)

    def r_copy(r, c):
        dst = ret.at[pl.ds(pl.multiple_of(r * CAP + c * CHUNK, CHUNK), CHUNK)]
        return remote(rsend.at[c, unit(0, r)], dst, r_ssem.at[r, c], r_rsem.at[r, c], along[r])

    for c in range(PARTS):
        for r in (1, 2, 3):
            z_copy(r, c).start()
        y_copy(0, c).start()

    for c in range(PARTS):
        xb[c, core, 0:CHUNK, :] = pk[0, c * CHUNK:(c + 1) * CHUNK, :]

    f0, f1 = fixed[0:1, :].astype(F32), fixed[1:2, :].astype(F32)
    s0, s1 = f0 / (f0 + f1), f1 / (f0 + f1)
    diag = (lax.broadcasted_iota(jnp.int32, (rows, rows), 0)
            == lax.broadcasted_iota(jnp.int32, (rows, rows), 1))

    def column(row):
        return jnp.sum(jnp.where(diag, row, 0.0), axis=1, keepdims=True)

    lane = lax.broadcasted_iota(jnp.int32, (rows, EXPERTS * CAP), 1).astype(F32)
    weigh = jnp.zeros((rows, EXPERTS * CAP), F32)
    for r in range(EXPERTS):
        e = flip(r)
        share = jnp.where(i0 == e, s0, 0.0) + jnp.where(i1 == e, s1, 0.0)
        place = column(jnp.where(match[r] > 0.0, pos[r:r + 1, :] + float(r * CAP), -1.0))
        weigh = weigh + jnp.where(place == lane, column(share), 0.0)
    high = weigh.astype(BF16)
    pick[0:rows, :] = high
    pick[rows:2 * rows, :] = (weigh - high.astype(F32)).astype(BF16)

    def relay(c):
        for r in (1, 2, 3):
            z_copy(r, c).wait_recv()
            y_copy(r, c).start()
        b_copy(0, c).start()

    def spread(c):
        for r in range(EXPERTS):
            y_copy(r, c).wait_recv()
        b_copy(1, c).start()

    def to_partner(c):
        k_copy(c).wait_recv()
        for r in (3, 2, 1, 0):
            piece = pl.ds(block + r * CHUNK, CHUNK)
            psend[c, unit(0, r), :] = (yown[c, piece, :] + zin[c, piece, :].astype(F32)).astype(BF16)
            p_copy(r, c).start()

    def to_origin(c):
        for r in (3, 2, 1, 0):
            p_copy(r, c).wait_recv()
            piece = unit(0, r)
            total = (yown[c, piece, :] + zin[c, piece, :].astype(F32)
                     + precv[c, piece, :].astype(F32)).astype(BF16)
            if r == 0:
                ret[slots(c), :] = total
            else:
                rsend[c, piece, :] = total
                r_copy(r, c).start()

    relay(0)
    spread(0)

    def step(c, carry):
        b_copy(0, c).wait_recv()
        b_copy(1, c).wait_recv()

        @pl.when(c < PARTS - 1)
        def _():
            relay(c + 1)

        for j in range(tiles):
            @pl.when(c == 0)
            def _():
                for copy in weight_copies(j):
                    copy.wait()

            cols = pl.ds(j * tile, tile)
            a, b = xb[c, 0], xb[c, 1]
            g = (jnp.dot(a, vg[0:half, cols], preferred_element_type=F32)
                 + jnp.dot(b, vg[half:2 * half, cols], preferred_element_type=F32))
            u = (jnp.dot(a, vu[0:half, cols], preferred_element_type=F32)
                 + jnp.dot(b, vu[half:2 * half, cols], preferred_element_type=F32))
            hid[:, cols] = (g / (1.0 + jnp.exp(-g)) * u).astype(BF16)
            if j == 0:
                @pl.when(c > 0)
                def _():
                    to_partner(c - 1)

        @pl.when(c < PARTS - 1)
        def _():
            spread(c + 1)

        @pl.when(c > 0)
        def _():
            to_origin(c - 1)

        def down(which):
            @pl.when(c == 0)
            def _():
                down_copy(which).wait()

            cols = pl.ds(pl.multiple_of(which * half, half), half)
            return jnp.dot(hid[...], vd[:, cols], preferred_element_type=F32)

        ysend[c] = down(other).astype(BF16)
        k_copy(c).start()
        yown[c] = down(core)
        return carry

    lax.fori_loop(0, PARTS, step, 0)
    to_partner(PARTS - 1)
    to_origin(PARTS - 1)

    for c in range(PARTS):
        for r in (1, 2, 3):
            r_copy(r, c).wait_recv()
    mixed = jnp.dot(pick[...], ret[...], preferred_element_type=F32)
    out[...] = (mixed[0:rows] + mixed[rows:2 * rows]).astype(BF16)

    def drain(c, carry):
        for r in range(EXPERTS):
            if r:
                z_copy(r, c).wait_send()
                r_copy(r, c).wait_send()
            y_copy(r, c).wait_send()
            p_copy(r, c).wait_send()
        for q in range(2):
            b_copy(q, c).wait_send()
        k_copy(c).wait_send()
        return carry

    lax.fori_loop(0, PARTS, drain, 0)


def slot_per_device(tokens, expert_ids, gate_fixed, gate_weight, up_weight, down_weight):
    rows, half = tokens.shape
    ff = gate_weight.shape[2]
    tiles = ff // min(GU_TILE, ff)
    many = 2 * EXPERTS * CHUNK
    dma = pltpu.SemaphoreType.DMA
    vmem = pl.BlockSpec(memory_space=pltpu.VMEM)
    hbm = pl.BlockSpec(memory_space=pl.ANY)
    return pl.pallas_call(
        slot_kernel,
        out_shape=jax.ShapeDtypeStruct((rows, half), BF16),
        in_specs=[vmem, vmem, vmem, hbm, hbm, hbm],
        out_specs=vmem,
        scratch_shapes=[
            pltpu.VMEM((EXPERTS, CAP, half), BF16),
            pltpu.VMEM((PARTS, 2, many, half), BF16),
            pltpu.VMEM((many, ff), BF16),
            pltpu.VMEM((PARTS, many, half), F32),
            pltpu.VMEM((PARTS, many, half), BF16),
            pltpu.VMEM((PARTS, many, half), BF16),
            pltpu.VMEM((PARTS, many // 2, half), BF16),
            pltpu.VMEM((PARTS, many // 2, half), BF16),
            pltpu.VMEM((PARTS, many // 2, half), BF16),
            pltpu.VMEM((EXPERTS * CAP, half), BF16),
            pltpu.VMEM((2 * rows, EXPERTS * CAP), BF16),
            pltpu.VMEM((2 * half, ff), BF16),
            pltpu.VMEM((2 * half, ff), BF16),
            pltpu.VMEM((ff, 2 * half), BF16),
            dma((tiles,)), dma((tiles,)), dma((2,)),
            dma((EXPERTS, PARTS)), dma((EXPERTS, PARTS)),
            dma((EXPERTS, PARTS)), dma((EXPERTS, PARTS)),
            dma((2, PARTS)), dma((2, PARTS)),
            dma((PARTS,)), dma((PARTS,)),
            dma((EXPERTS, PARTS)), dma((EXPERTS, PARTS)),
            dma((EXPERTS, PARTS)), dma((EXPERTS, PARTS)),
        ],
        compiler_params=pltpu.CompilerParams(
            collective_id=0, has_side_effects=True, vmem_limit_bytes=60 * 1024 * 1024),
    )(tokens, expert_ids.T, gate_fixed.T, gate_weight, up_weight, down_weight)


def solution(mesh):
    placed = (
        P(("group", "expert"), "tensor"),
        P(("group", "expert"), None),
        P(("group", "expert"), None),
        P("expert", None, "tensor"),
        P("expert", None, "tensor"),
        P("expert", "tensor", None),
    )
    return jax.shard_map(
        slot_per_device if mesh.shape["expert"] == 2 * EXPERTS else ring_per_device,
        mesh=mesh,
        in_specs=placed,
        out_specs=P(("group", "expert"), "tensor"),
        check_vma=False,
    )
```

```python
import functools

import jax
import jax.numpy as jnp
from jax import lax
from jax.experimental import pallas as pl
from jax.experimental.pallas import tpu as pltpu
from jax.sharding import PartitionSpec as P

EXPERTS = 4
TILE = 1024
DOWN_TILE = 768
F32 = jnp.float32
BF16 = jnp.bfloat16


def ring_kernel(n, tok, ids, fixed, wg, wu, wd, out,
           xb, wt, hid, yown, ysend, zin, psend, precv, vg, vu, vd,
           g_sem, u_sem, d_sem, x_ssem, x_rsem, w_ssem, w_rsem, b_ssem, b_rsem,
           z_ssem, z_rsem, p_ssem, p_rsem):
    h = n // 2
    rows, half = tok.shape
    part = rows // 2
    me = lax.axis_index("expert")
    core = lax.axis_index("tensor")
    other = 1 - core
    expert = me // (n // EXPERTS)
    odd = me % 2
    pos = (1 - odd) * (me // 2) + odd * (n - 1 - me // 2)

    def at_pos(p):
        p = (p + n) % n
        back = p // h
        return (1 - back) * (2 * p) + back * (2 * (n - 1 - p) + 1)

    onward = ({"expert": at_pos(pos + 1)}, {"expert": at_pos(pos - 1)})
    sibling = {"tensor": other}

    ff = hid.shape[1]
    tile = min(TILE, ff)
    j_hidden = ff // tile
    j_half = half // DOWN_TILE

    def hidden_cols(j):
        return pl.ds(pl.multiple_of(j * tile, tile), tile)

    def out_cols(j):
        return pl.ds(pl.multiple_of(j * DOWN_TILE, DOWN_TILE), DOWN_TILE)

    def weight_copies(j):
        cols = hidden_cols(j)
        return (pltpu.make_async_copy(wg.at[0, :, cols], vg.at[:, cols], g_sem.at[j]),
                pltpu.make_async_copy(wu.at[0, :, cols], vu.at[:, cols], u_sem.at[j]))

    def down_copy(j):
        cols = out_cols(j)
        return pltpu.make_async_copy(wd.at[0, :, cols], vd.at[:, cols], d_sem.at[j])

    @pl.loop(0, j_hidden)
    def _(j):
        for copy in weight_copies(j):
            copy.start()

    @pl.loop(0, 2 * j_half)
    def _(j):
        down_copy(j).start()

    barrier = pltpu.get_barrier_semaphore()
    for target in onward + (sibling,):
        pl.semaphore_signal(barrier, inc=1, device_id=target, device_id_type=pl.DeviceIdType.MESH)

    diag = (lax.broadcasted_iota(jnp.int32, (rows, 128), 0)
            == lax.broadcasted_iota(jnp.int32, (rows, 128), 1))
    f0 = fixed[:, 0:1].astype(F32)
    f1 = fixed[:, 1:2].astype(F32)
    total = f0 + f1
    s0, s1 = f0 / total, f1 / total
    i0, i1 = ids[:, 0:1], ids[:, 1:2]
    wt[0, 0] = jnp.zeros((8, 128), F32)
    for e in range(EXPERTS):
        col = jnp.where(i0 == e, s0, 0.0) + jnp.where(i1 == e, s1, 0.0)
        wt[0, 0, e:e + 1, :] = jnp.sum(jnp.where(diag, col, 0.0), axis=0, keepdims=True)
    xb[0, core, 0:rows, :] = tok[...]
    pl.semaphore_wait(barrier, 3)

    def remote(src, dst, ssem, rsem, target):
        return pltpu.make_async_remote_copy(
            src_ref=src, dst_ref=dst, send_sem=ssem, recv_sem=rsem,
            device_id=target, device_id_type=pl.DeviceIdType.MESH)

    def x_copy(d, s, q):
        piece = pl.ds(d * rows + q * part, part)
        return remote(xb.at[s - 1, core, piece], xb.at[s, core, piece],
                      x_ssem.at[d, s, q], x_rsem.at[d, s, q], onward[d])

    def x_first(d, q):
        return remote(xb.at[0, core, pl.ds(q * part, part)],
                      xb.at[1, core, pl.ds(d * rows + q * part, part)],
                      x_ssem.at[d, 1, q], x_rsem.at[d, 1, q], onward[d])

    def x_last(d):
        return remote(xb.at[h - 1, core, pl.ds(d * rows + d * part, part)],
                      xb.at[0, core, pl.ds(rows + d * part, part)],
                      x_ssem.at[d, h, d], x_rsem.at[d, h, d], onward[d])

    def w_copy(d, s):
        return remote(wt.at[s - 1, d], wt.at[s, d], w_ssem.at[d, s], w_rsem.at[d, s], onward[d])

    def w_first(d):
        return remote(wt.at[0, 0], wt.at[1, d], w_ssem.at[d, 1], w_rsem.at[d, 1], onward[d])

    def w_last():
        return remote(wt.at[h - 1, 0], wt.at[0, 1], w_ssem.at[0, h], w_rsem.at[0, h], onward[0])

    def b_copy(d, s):
        place = xb.at[s, core, pl.ds(d * rows, rows)]
        return remote(place, place, b_ssem.at[d, s], b_rsem.at[d, s], sibling)

    def z_copy(s):
        return remote(ysend.at[s], zin.at[s], z_ssem.at[s], z_rsem.at[s], sibling)

    for d in range(2):
        w_first(d).start()
    for q in range(2):
        for d in range(2):
            x_first(d, d if q == 0 else 1 - d).start()
    b_copy(0, 0).start()

    def compute(s, first):
        @pl.loop(0, j_hidden)
        def _(j):
            cols = hidden_cols(j)

            @pl.when(first)
            def _():
                for copy in weight_copies(j):
                    copy.wait()

            a, b = xb[s, 0], xb[s, 1]
            g = (jnp.dot(a, vg[0:half, cols], preferred_element_type=F32)
                 + jnp.dot(b, vg[half:2 * half, cols], preferred_element_type=F32))
            u = (jnp.dot(a, vu[0:half, cols], preferred_element_type=F32)
                 + jnp.dot(b, vu[half:2 * half, cols], preferred_element_type=F32))
            hid[:, cols] = (g / (1.0 + jnp.exp(-g)) * u).astype(BF16)

        share = jnp.concatenate(
            [jnp.sum(jnp.where(diag, wt[s, d, pl.ds(expert, 1), :], 0.0), axis=1, keepdims=True)
             for d in range(2)], axis=0)

        def down(j, which):
            cols = pl.ds(pl.multiple_of(which * half + j * DOWN_TILE, DOWN_TILE), DOWN_TILE)

            @pl.when(first)
            def _():
                down_copy(which * j_half + j).wait()

            return jnp.dot(hid[...], vd[:, cols], preferred_element_type=F32) * share

        @pl.loop(0, j_half)
        def _(j):
            ysend[s, :, out_cols(j)] = down(j, other).astype(BF16)

        z_copy(s).start()

        @pl.loop(0, j_half)
        def _(j):
            yown[s, :, out_cols(j)] = down(j, core)

    def step(s, carry):
        for turn in range(2):
            for d in range(2):
                q = d if turn == 0 else 1 - d
                x_copy(d, s, q).wait_recv()

                @pl.when(s < h - 1)
                def _():
                    x_copy(d, s + 1, q).start()

                if turn == 0:
                    @pl.when(s == h - 1)
                    def _():
                        x_last(d).start()

        for d in range(2):
            w_copy(d, s).wait_recv()

        @pl.when(s < h - 1)
        def _():
            for d in range(2):
                w_copy(d, s + 1).start()

        @pl.when(s == h - 1)
        def _():
            w_last().start()

        for d in range(2):
            b_copy(d, s).start()
        for d in range(2):
            b_copy(d, s).wait_recv()
        compute(s, s == 1)
        return carry

    lax.fori_loop(1, h, step, 0)
    for d in range(2):
        x_last(d).wait_recv()
    w_last().wait_recv()
    b_copy(1, 0).start()
    b_copy(0, 0).wait_recv()
    b_copy(1, 0).wait_recv()
    compute(0, False)

    def p_copy(d, k, q):
        piece = pl.ds(q * part, part)
        return remote(psend.at[d, k, piece], precv.at[d, k, piece],
                      p_ssem.at[d, k, q], p_rsem.at[d, k, q], onward[d])

    z_copy(0).wait_recv()
    for k in range(h, 0, -1):
        slot = k % h
        if k < h:
            z_copy(k).wait_recv()
        for turn in range(2):
            for d in range(2):
                q = (1 - d) if turn == 0 else d
                if k == h and q != d:
                    continue
                base = (rows if k == h or d == 0 else 0) + q * part
                total = yown[slot, base:base + part, :] + zin[slot, base:base + part, :].astype(F32)
                if k < h - 1 or (k == h - 1 and q == d):
                    p_copy(d, k, q).wait_recv()
                    total = total + precv[d, k, q * part:(q + 1) * part, :].astype(F32)
                psend[d, k - 1, q * part:(q + 1) * part, :] = total.astype(BF16)
                p_copy(d, k - 1, q).start()
    for q in (0, 1):
        total = yown[0, q * part:(q + 1) * part, :] + zin[0, q * part:(q + 1) * part, :].astype(F32)
        for d in range(2):
            p_copy(d, 0, q).wait_recv()
            total = total + precv[d, 0, q * part:(q + 1) * part, :].astype(F32)
        out[q * part:(q + 1) * part, :] = total.astype(BF16)

    for d in range(2):
        for q in range(2):
            x_first(d, q).wait_send()
        w_first(d).wait_send()
        x_last(d).wait_send()
        for k in range(h):
            for q in range(2):
                if k < h - 1 or q == d:
                    p_copy(d, k, q).wait_send()
    w_last().wait_send()

    def drain(s, carry):
        for d in range(2):
            for q in range(2):
                x_copy(d, s, q).wait_send()
            w_copy(d, s).wait_send()
        return carry

    lax.fori_loop(2, h, drain, 0)

    def drain_sibling(s, carry):
        for d in range(2):
            b_copy(d, s).wait_send()
        z_copy(s).wait_send()
        return carry

    lax.fori_loop(0, h, drain_sibling, 0)


def ring_per_device(tokens, expert_ids, gate_fixed, gate_weight, up_weight, down_weight):
    n = lax.axis_size("expert")
    h = n // 2
    rows, half = tokens.shape
    ff = gate_weight.shape[2]
    dma = pltpu.SemaphoreType.DMA
    vmem = pl.BlockSpec(memory_space=pltpu.VMEM)
    hbm = pl.BlockSpec(memory_space=pl.ANY)
    return pl.pallas_call(
        functools.partial(ring_kernel, n),
        out_shape=jax.ShapeDtypeStruct((rows, half), BF16),
        in_specs=[vmem, vmem, vmem, hbm, hbm, hbm],
        out_specs=vmem,
        scratch_shapes=[
            pltpu.VMEM((h, 2, 2 * rows, half), BF16),
            pltpu.VMEM((h, 2, 8, 128), F32),
            pltpu.VMEM((2 * rows, ff), BF16),
            pltpu.VMEM((h, 2 * rows, half), F32),
            pltpu.VMEM((h, 2 * rows, half), BF16),
            pltpu.VMEM((h, 2 * rows, half), BF16),
            pltpu.VMEM((2, h, rows, half), BF16),
            pltpu.VMEM((2, h, rows, half), BF16),
            pltpu.VMEM((2 * half, ff), BF16),
            pltpu.VMEM((2 * half, ff), BF16),
            pltpu.VMEM((ff, 2 * half), BF16),
            dma((ff // min(TILE, ff),)), dma((ff // min(TILE, ff),)), dma((2 * half // DOWN_TILE,)),
            dma((2, h + 1, 2)), dma((2, h + 1, 2)),
            dma((2, h + 1)), dma((2, h + 1)),
            dma((2, h)), dma((2, h)),
            dma((h,)), dma((h,)),
            dma((2, h, 2)), dma((2, h, 2)),
        ],
        compiler_params=pltpu.CompilerParams(
            collective_id=0, has_side_effects=True, vmem_limit_bytes=60 * 1024 * 1024),
    )(tokens, expert_ids, gate_fixed, gate_weight, up_weight, down_weight)


CAP = 48
CHUNK = 16
PARTS = CAP // CHUNK
GU_TILE = 1024


def slot_kernel(tok, ids, fixed, wg, wu, wd, out,
                pk, xb, hid, yown, ysend, zin, psend, precv, rsend, ret, pick, vg, vu, vd,
                g_sem, u_sem, d_sem, z_ssem, z_rsem, y_ssem, y_rsem, b_ssem, b_rsem,
                k_ssem, k_rsem, p_ssem, p_rsem, r_ssem, r_rsem):
    rows, half = tok.shape
    ff = hid.shape[1]
    block = EXPERTS * CHUNK
    me = lax.axis_index("expert")
    core = lax.axis_index("tensor")
    other = 1 - core
    z, y = me // 2, me % 2

    def flip(r):
        hi = z // 2 if r < 2 else 1 - z // 2
        lo = z % 2 if r % 2 == 0 else 1 - z % 2
        return 2 * hi + lo

    sibling = {"tensor": other}
    across = {"expert": 2 * z + 1 - y}
    along = {r: {"expert": 2 * flip(r) + y} for r in range(1, EXPERTS)}

    barrier = pltpu.get_barrier_semaphore()
    for target in (*along.values(), across, sibling):
        pl.semaphore_signal(barrier, inc=1, device_id=target, device_id_type=pl.DeviceIdType.MESH)

    tile = min(GU_TILE, ff)
    tiles = ff // tile

    def weight_copies(j):
        cols = pl.ds(j * tile, tile)
        return (pltpu.make_async_copy(wg.at[0, :, cols], vg.at[:, cols], g_sem.at[j]),
                pltpu.make_async_copy(wu.at[0, :, cols], vu.at[:, cols], u_sem.at[j]))

    def down_copy(which):
        cols = pl.ds(pl.multiple_of(which * half, half), half)
        return pltpu.make_async_copy(wd.at[0, :, cols], vd.at[:, cols], d_sem.at[which])

    for j in range(tiles):
        for copy in weight_copies(j):
            copy.start()
    down_copy(other).start()
    down_copy(core).start()

    i0, i1 = ids[0:1, :], ids[1:2, :]
    match = [jnp.where((i0 == flip(r)) | (i1 == flip(r)), 1.0, 0.0) for r in range(EXPERTS)]
    before = (lax.broadcasted_iota(jnp.int32, (rows, rows), 0)
              < lax.broadcasted_iota(jnp.int32, (rows, rows), 1))
    stacked = jnp.concatenate(match + [jnp.zeros((8 - EXPERTS, rows), F32)], axis=0)
    pos = jnp.dot(stacked.astype(BF16), jnp.where(before, 1.0, 0.0).astype(BF16),
                  preferred_element_type=F32)
    slot = [jnp.where(match[r] > 0.0, pos[r:r + 1, :], -1.0) for r in range(EXPERTS)]
    number = lax.broadcasted_iota(jnp.int32, (CAP, rows), 0).astype(F32)
    for r in range(EXPERTS):
        chosen = jnp.where(slot[r] == number, 1.0, 0.0).astype(BF16)
        pk[r] = jnp.dot(chosen, tok[...], preferred_element_type=F32).astype(BF16)
    pl.semaphore_wait(barrier, EXPERTS + 1)

    def remote(src, dst, ssem, rsem, target):
        return pltpu.make_async_remote_copy(
            src_ref=src, dst_ref=dst, send_sem=ssem, recv_sem=rsem,
            device_id=target, device_id_type=pl.DeviceIdType.MESH)

    def slots(c):
        return pl.ds(pl.multiple_of(c * CHUNK, CHUNK), CHUNK)

    def unit(q, r):
        return pl.ds(q * block + r * CHUNK, CHUNK)

    def z_copy(r, c):
        return remote(pk.at[r, slots(c)], xb.at[c, core, unit(0, r)],
                      z_ssem.at[r, c], z_rsem.at[r, c], along[r])

    def y_copy(r, c):
        src = pk.at[0, slots(c)] if r == 0 else xb.at[c, core, unit(0, r)]
        return remote(src, xb.at[c, core, unit(1, r)], y_ssem.at[r, c], y_rsem.at[r, c], across)

    def b_copy(q, c):
        place = xb.at[c, core, pl.ds(q * block, block)]
        return remote(place, place, b_ssem.at[q, c], b_rsem.at[q, c], sibling)

    def k_copy(c):
        return remote(ysend.at[c], zin.at[c], k_ssem.at[c], k_rsem.at[c], sibling)

    def p_copy(r, c):
        return remote(psend.at[c, unit(0, r)], precv.at[c, unit(0, r)],
                      p_ssem.at[r, c], p_rsem.at[r, c], across)

    def r_copy(r, c):
        dst = ret.at[pl.ds(pl.multiple_of(r * CAP + c * CHUNK, CHUNK), CHUNK)]
        return remote(rsend.at[c, unit(0, r)], dst, r_ssem.at[r, c], r_rsem.at[r, c], along[r])

    for c in range(PARTS):
        for r in (1, 2, 3):
            z_copy(r, c).start()
        y_copy(0, c).start()

    for c in range(PARTS):
        xb[c, core, 0:CHUNK, :] = pk[0, c * CHUNK:(c + 1) * CHUNK, :]

    f0, f1 = fixed[0:1, :].astype(F32), fixed[1:2, :].astype(F32)
    s0, s1 = f0 / (f0 + f1), f1 / (f0 + f1)
    diag = (lax.broadcasted_iota(jnp.int32, (rows, rows), 0)
            == lax.broadcasted_iota(jnp.int32, (rows, rows), 1))

    def column(row):
        return jnp.sum(jnp.where(diag, row, 0.0), axis=1, keepdims=True)

    lane = lax.broadcasted_iota(jnp.int32, (rows, EXPERTS * CAP), 1).astype(F32)
    weigh = jnp.zeros((rows, EXPERTS * CAP), F32)
    for r in range(EXPERTS):
        e = flip(r)
        share = jnp.where(i0 == e, s0, 0.0) + jnp.where(i1 == e, s1, 0.0)
        place = column(jnp.where(match[r] > 0.0, pos[r:r + 1, :] + float(r * CAP), -1.0))
        weigh = weigh + jnp.where(place == lane, column(share), 0.0)
    high = weigh.astype(BF16)
    pick[0:rows, :] = high
    pick[rows:2 * rows, :] = (weigh - high.astype(F32)).astype(BF16)

    def relay(c):
        for r in (1, 2, 3):
            z_copy(r, c).wait_recv()
            y_copy(r, c).start()
        b_copy(0, c).start()

    def spread(c):
        for r in range(EXPERTS):
            y_copy(r, c).wait_recv()
        b_copy(1, c).start()

    def to_partner(c):
        k_copy(c).wait_recv()
        for r in (3, 2, 1, 0):
            piece = pl.ds(block + r * CHUNK, CHUNK)
            psend[c, unit(0, r), :] = (yown[c, piece, :] + zin[c, piece, :].astype(F32)).astype(BF16)
            p_copy(r, c).start()

    def to_origin(c, r):
        p_copy(r, c).wait_recv()
        piece = unit(0, r)
        total = (yown[c, piece, :] + zin[c, piece, :].astype(F32)
                 + precv[c, piece, :].astype(F32)).astype(BF16)
        if r == 0:
            ret[slots(c), :] = total
        else:
            rsend[c, piece, :] = total
            r_copy(r, c).start()

    relay(0)
    spread(0)
    relay(1)

    def step(c, carry):
        b_copy(0, c).wait_recv()
        b_copy(1, c).wait_recv()

        @pl.when(c > 1)
        def _():
            to_origin(c - 2, 3)

        for j in range(tiles):
            @pl.when(c == 0)
            def _():
                for copy in weight_copies(j):
                    copy.wait()

            cols = pl.ds(j * tile, tile)
            a, b = xb[c, 0], xb[c, 1]
            g = (jnp.dot(a, vg[0:half, cols], preferred_element_type=F32)
                 + jnp.dot(b, vg[half:2 * half, cols], preferred_element_type=F32))
            u = (jnp.dot(a, vu[0:half, cols], preferred_element_type=F32)
                 + jnp.dot(b, vu[half:2 * half, cols], preferred_element_type=F32))
            hid[:, cols] = (g / (1.0 + jnp.exp(-g)) * u).astype(BF16)
            if j == 0:
                @pl.when(c > 0)
                def _():
                    to_partner(c - 1)

                @pl.when(c > 1)
                def _():
                    to_origin(c - 2, 2)

        @pl.when(c < PARTS - 2)
        def _():
            relay(c + 2)

        @pl.when(c > 1)
        def _():
            to_origin(c - 2, 1)
            to_origin(c - 2, 0)

        def down(which):
            @pl.when(c == 0)
            def _():
                down_copy(which).wait()

            cols = pl.ds(pl.multiple_of(which * half, half), half)
            return jnp.dot(hid[...], vd[:, cols], preferred_element_type=F32)

        ysend[c] = down(other).astype(BF16)
        k_copy(c).start()

        @pl.when(c < PARTS - 1)
        def _():
            spread(c + 1)

        yown[c] = down(core)
        return carry

    lax.fori_loop(0, PARTS, step, 0)
    to_origin(PARTS - 2, 3)
    to_partner(PARTS - 1)
    for r in (2, 1, 0):
        to_origin(PARTS - 2, r)
    for r in (3, 2, 1, 0):
        to_origin(PARTS - 1, r)

    for c in range(PARTS):
        for r in (1, 2, 3):
            r_copy(r, c).wait_recv()
    mixed = jnp.dot(pick[...], ret[...], preferred_element_type=F32)
    out[...] = (mixed[0:rows] + mixed[rows:2 * rows]).astype(BF16)

    def drain(c, carry):
        for r in range(EXPERTS):
            if r:
                z_copy(r, c).wait_send()
                r_copy(r, c).wait_send()
            y_copy(r, c).wait_send()
            p_copy(r, c).wait_send()
        for q in range(2):
            b_copy(q, c).wait_send()
        k_copy(c).wait_send()
        return carry

    lax.fori_loop(0, PARTS, drain, 0)


def slot_per_device(tokens, expert_ids, gate_fixed, gate_weight, up_weight, down_weight):
    rows, half = tokens.shape
    ff = gate_weight.shape[2]
    tiles = ff // min(GU_TILE, ff)
    many = 2 * EXPERTS * CHUNK
    dma = pltpu.SemaphoreType.DMA
    vmem = pl.BlockSpec(memory_space=pltpu.VMEM)
    hbm = pl.BlockSpec(memory_space=pl.ANY)
    return pl.pallas_call(
        slot_kernel,
        out_shape=jax.ShapeDtypeStruct((rows, half), BF16),
        in_specs=[vmem, vmem, vmem, hbm, hbm, hbm],
        out_specs=vmem,
        scratch_shapes=[
            pltpu.VMEM((EXPERTS, CAP, half), BF16),
            pltpu.VMEM((PARTS, 2, many, half), BF16),
            pltpu.VMEM((many, ff), BF16),
            pltpu.VMEM((PARTS, many, half), F32),
            pltpu.VMEM((PARTS, many, half), BF16),
            pltpu.VMEM((PARTS, many, half), BF16),
            pltpu.VMEM((PARTS, many // 2, half), BF16),
            pltpu.VMEM((PARTS, many // 2, half), BF16),
            pltpu.VMEM((PARTS, many // 2, half), BF16),
            pltpu.VMEM((EXPERTS * CAP, half), BF16),
            pltpu.VMEM((2 * rows, EXPERTS * CAP), BF16),
            pltpu.VMEM((2 * half, ff), BF16),
            pltpu.VMEM((2 * half, ff), BF16),
            pltpu.VMEM((ff, 2 * half), BF16),
            dma((tiles,)), dma((tiles,)), dma((2,)),
            dma((EXPERTS, PARTS)), dma((EXPERTS, PARTS)),
            dma((EXPERTS, PARTS)), dma((EXPERTS, PARTS)),
            dma((2, PARTS)), dma((2, PARTS)),
            dma((PARTS,)), dma((PARTS,)),
            dma((EXPERTS, PARTS)), dma((EXPERTS, PARTS)),
            dma((EXPERTS, PARTS)), dma((EXPERTS, PARTS)),
        ],
        compiler_params=pltpu.CompilerParams(
            collective_id=0, has_side_effects=True, vmem_limit_bytes=60 * 1024 * 1024),
    )(tokens, expert_ids.T, gate_fixed.T, gate_weight, up_weight, down_weight)


def solution(mesh):
    placed = (
        P(("group", "expert"), "tensor"),
        P(("group", "expert"), None),
        P(("group", "expert"), None),
        P("expert", None, "tensor"),
        P("expert", None, "tensor"),
        P("expert", "tensor", None),
    )
    return jax.shard_map(
        slot_per_device if mesh.shape["expert"] == 2 * EXPERTS else ring_per_device,
        mesh=mesh,
        in_specs=placed,
        out_specs=P(("group", "expert"), "tensor"),
        check_vma=False,
    )
```

```python
import functools

import jax
import jax.numpy as jnp
from jax import lax
from jax.experimental import pallas as pl
from jax.experimental.pallas import tpu as pltpu
from jax.sharding import PartitionSpec as P

EXPERTS = 4
TILE = 1024
DOWN_TILE = 768
F32 = jnp.float32
BF16 = jnp.bfloat16


def ring_kernel(n, tok, ids, fixed, wg, wu, wd, out,
           xb, wt, hid, yown, ysend, zin, psend, precv, vg, vu, vd,
           g_sem, u_sem, d_sem, x_ssem, x_rsem, w_ssem, w_rsem, b_ssem, b_rsem,
           z_ssem, z_rsem, p_ssem, p_rsem):
    h = n // 2
    rows, half = tok.shape
    part = rows // 2
    me = lax.axis_index("expert")
    core = lax.axis_index("tensor")
    other = 1 - core
    expert = me // (n // EXPERTS)
    odd = me % 2
    pos = (1 - odd) * (me // 2) + odd * (n - 1 - me // 2)

    def at_pos(p):
        p = (p + n) % n
        back = p // h
        return (1 - back) * (2 * p) + back * (2 * (n - 1 - p) + 1)

    onward = ({"expert": at_pos(pos + 1)}, {"expert": at_pos(pos - 1)})
    sibling = {"tensor": other}

    ff = hid.shape[1]
    tile = min(TILE, ff)
    j_hidden = ff // tile
    j_half = half // DOWN_TILE

    def hidden_cols(j):
        return pl.ds(pl.multiple_of(j * tile, tile), tile)

    def out_cols(j):
        return pl.ds(pl.multiple_of(j * DOWN_TILE, DOWN_TILE), DOWN_TILE)

    def weight_copies(j):
        cols = hidden_cols(j)
        return (pltpu.make_async_copy(wg.at[0, :, cols], vg.at[:, cols], g_sem.at[j]),
                pltpu.make_async_copy(wu.at[0, :, cols], vu.at[:, cols], u_sem.at[j]))

    def down_copy(j):
        cols = out_cols(j)
        return pltpu.make_async_copy(wd.at[0, :, cols], vd.at[:, cols], d_sem.at[j])

    @pl.loop(0, j_hidden)
    def _(j):
        for copy in weight_copies(j):
            copy.start()

    @pl.loop(0, 2 * j_half)
    def _(j):
        down_copy(j).start()

    barrier = pltpu.get_barrier_semaphore()
    for target in onward + (sibling,):
        pl.semaphore_signal(barrier, inc=1, device_id=target, device_id_type=pl.DeviceIdType.MESH)

    diag = (lax.broadcasted_iota(jnp.int32, (rows, 128), 0)
            == lax.broadcasted_iota(jnp.int32, (rows, 128), 1))
    f0 = fixed[:, 0:1].astype(F32)
    f1 = fixed[:, 1:2].astype(F32)
    total = f0 + f1
    s0, s1 = f0 / total, f1 / total
    i0, i1 = ids[:, 0:1], ids[:, 1:2]
    wt[0, 0] = jnp.zeros((8, 128), F32)
    for e in range(EXPERTS):
        col = jnp.where(i0 == e, s0, 0.0) + jnp.where(i1 == e, s1, 0.0)
        wt[0, 0, e:e + 1, :] = jnp.sum(jnp.where(diag, col, 0.0), axis=0, keepdims=True)
    xb[0, core, 0:rows, :] = tok[...]
    pl.semaphore_wait(barrier, 3)

    def remote(src, dst, ssem, rsem, target):
        return pltpu.make_async_remote_copy(
            src_ref=src, dst_ref=dst, send_sem=ssem, recv_sem=rsem,
            device_id=target, device_id_type=pl.DeviceIdType.MESH)

    def x_copy(d, s, q):
        piece = pl.ds(d * rows + q * part, part)
        return remote(xb.at[s - 1, core, piece], xb.at[s, core, piece],
                      x_ssem.at[d, s, q], x_rsem.at[d, s, q], onward[d])

    def x_first(d, q):
        return remote(xb.at[0, core, pl.ds(q * part, part)],
                      xb.at[1, core, pl.ds(d * rows + q * part, part)],
                      x_ssem.at[d, 1, q], x_rsem.at[d, 1, q], onward[d])

    def x_last(d):
        return remote(xb.at[h - 1, core, pl.ds(d * rows + d * part, part)],
                      xb.at[0, core, pl.ds(rows + d * part, part)],
                      x_ssem.at[d, h, d], x_rsem.at[d, h, d], onward[d])

    def w_copy(d, s):
        return remote(wt.at[s - 1, d], wt.at[s, d], w_ssem.at[d, s], w_rsem.at[d, s], onward[d])

    def w_first(d):
        return remote(wt.at[0, 0], wt.at[1, d], w_ssem.at[d, 1], w_rsem.at[d, 1], onward[d])

    def w_last():
        return remote(wt.at[h - 1, 0], wt.at[0, 1], w_ssem.at[0, h], w_rsem.at[0, h], onward[0])

    def b_copy(d, s):
        place = xb.at[s, core, pl.ds(d * rows, rows)]
        return remote(place, place, b_ssem.at[d, s], b_rsem.at[d, s], sibling)

    def z_copy(s):
        return remote(ysend.at[s], zin.at[s], z_ssem.at[s], z_rsem.at[s], sibling)

    for d in range(2):
        w_first(d).start()
    for q in range(2):
        for d in range(2):
            x_first(d, d if q == 0 else 1 - d).start()
    b_copy(0, 0).start()

    def compute(s, first):
        @pl.loop(0, j_hidden)
        def _(j):
            cols = hidden_cols(j)

            @pl.when(first)
            def _():
                for copy in weight_copies(j):
                    copy.wait()

            a, b = xb[s, 0], xb[s, 1]
            g = (jnp.dot(a, vg[0:half, cols], preferred_element_type=F32)
                 + jnp.dot(b, vg[half:2 * half, cols], preferred_element_type=F32))
            u = (jnp.dot(a, vu[0:half, cols], preferred_element_type=F32)
                 + jnp.dot(b, vu[half:2 * half, cols], preferred_element_type=F32))
            hid[:, cols] = (g / (1.0 + jnp.exp(-g)) * u).astype(BF16)

        share = jnp.concatenate(
            [jnp.sum(jnp.where(diag, wt[s, d, pl.ds(expert, 1), :], 0.0), axis=1, keepdims=True)
             for d in range(2)], axis=0)

        def down(j, which):
            cols = pl.ds(pl.multiple_of(which * half + j * DOWN_TILE, DOWN_TILE), DOWN_TILE)

            @pl.when(first)
            def _():
                down_copy(which * j_half + j).wait()

            return jnp.dot(hid[...], vd[:, cols], preferred_element_type=F32) * share

        @pl.loop(0, j_half)
        def _(j):
            ysend[s, :, out_cols(j)] = down(j, other).astype(BF16)

        z_copy(s).start()

        @pl.loop(0, j_half)
        def _(j):
            yown[s, :, out_cols(j)] = down(j, core)

    def step(s, carry):
        for turn in range(2):
            for d in range(2):
                q = d if turn == 0 else 1 - d
                x_copy(d, s, q).wait_recv()

                @pl.when(s < h - 1)
                def _():
                    x_copy(d, s + 1, q).start()

                if turn == 0:
                    @pl.when(s == h - 1)
                    def _():
                        x_last(d).start()

        for d in range(2):
            w_copy(d, s).wait_recv()

        @pl.when(s < h - 1)
        def _():
            for d in range(2):
                w_copy(d, s + 1).start()

        @pl.when(s == h - 1)
        def _():
            w_last().start()

        for d in range(2):
            b_copy(d, s).start()
        for d in range(2):
            b_copy(d, s).wait_recv()
        compute(s, s == 1)
        return carry

    lax.fori_loop(1, h, step, 0)
    for d in range(2):
        x_last(d).wait_recv()
    w_last().wait_recv()
    b_copy(1, 0).start()
    b_copy(0, 0).wait_recv()
    b_copy(1, 0).wait_recv()
    compute(0, False)

    def p_copy(d, k, q):
        piece = pl.ds(q * part, part)
        return remote(psend.at[d, k, piece], precv.at[d, k, piece],
                      p_ssem.at[d, k, q], p_rsem.at[d, k, q], onward[d])

    z_copy(0).wait_recv()
    for k in range(h, 0, -1):
        slot = k % h
        if k < h:
            z_copy(k).wait_recv()
        for turn in range(2):
            for d in range(2):
                q = (1 - d) if turn == 0 else d
                if k == h and q != d:
                    continue
                base = (rows if k == h or d == 0 else 0) + q * part
                total = yown[slot, base:base + part, :] + zin[slot, base:base + part, :].astype(F32)
                if k < h - 1 or (k == h - 1 and q == d):
                    p_copy(d, k, q).wait_recv()
                    total = total + precv[d, k, q * part:(q + 1) * part, :].astype(F32)
                psend[d, k - 1, q * part:(q + 1) * part, :] = total.astype(BF16)
                p_copy(d, k - 1, q).start()
    for q in (0, 1):
        total = yown[0, q * part:(q + 1) * part, :] + zin[0, q * part:(q + 1) * part, :].astype(F32)
        for d in range(2):
            p_copy(d, 0, q).wait_recv()
            total = total + precv[d, 0, q * part:(q + 1) * part, :].astype(F32)
        out[q * part:(q + 1) * part, :] = total.astype(BF16)

    for d in range(2):
        for q in range(2):
            x_first(d, q).wait_send()
        w_first(d).wait_send()
        x_last(d).wait_send()
        for k in range(h):
            for q in range(2):
                if k < h - 1 or q == d:
                    p_copy(d, k, q).wait_send()
    w_last().wait_send()

    def drain(s, carry):
        for d in range(2):
            for q in range(2):
                x_copy(d, s, q).wait_send()
            w_copy(d, s).wait_send()
        return carry

    lax.fori_loop(2, h, drain, 0)

    def drain_sibling(s, carry):
        for d in range(2):
            b_copy(d, s).wait_send()
        z_copy(s).wait_send()
        return carry

    lax.fori_loop(0, h, drain_sibling, 0)


def ring_per_device(tokens, expert_ids, gate_fixed, gate_weight, up_weight, down_weight):
    n = lax.axis_size("expert")
    h = n // 2
    rows, half = tokens.shape
    ff = gate_weight.shape[2]
    dma = pltpu.SemaphoreType.DMA
    vmem = pl.BlockSpec(memory_space=pltpu.VMEM)
    hbm = pl.BlockSpec(memory_space=pl.ANY)
    return pl.pallas_call(
        functools.partial(ring_kernel, n),
        out_shape=jax.ShapeDtypeStruct((rows, half), BF16),
        in_specs=[vmem, vmem, vmem, hbm, hbm, hbm],
        out_specs=vmem,
        scratch_shapes=[
            pltpu.VMEM((h, 2, 2 * rows, half), BF16),
            pltpu.VMEM((h, 2, 8, 128), F32),
            pltpu.VMEM((2 * rows, ff), BF16),
            pltpu.VMEM((h, 2 * rows, half), F32),
            pltpu.VMEM((h, 2 * rows, half), BF16),
            pltpu.VMEM((h, 2 * rows, half), BF16),
            pltpu.VMEM((2, h, rows, half), BF16),
            pltpu.VMEM((2, h, rows, half), BF16),
            pltpu.VMEM((2 * half, ff), BF16),
            pltpu.VMEM((2 * half, ff), BF16),
            pltpu.VMEM((ff, 2 * half), BF16),
            dma((ff // min(TILE, ff),)), dma((ff // min(TILE, ff),)), dma((2 * half // DOWN_TILE,)),
            dma((2, h + 1, 2)), dma((2, h + 1, 2)),
            dma((2, h + 1)), dma((2, h + 1)),
            dma((2, h)), dma((2, h)),
            dma((h,)), dma((h,)),
            dma((2, h, 2)), dma((2, h, 2)),
        ],
        compiler_params=pltpu.CompilerParams(
            collective_id=0, has_side_effects=True, vmem_limit_bytes=60 * 1024 * 1024),
    )(tokens, expert_ids, gate_fixed, gate_weight, up_weight, down_weight)


CAP = 48
CHUNK = 16
PARTS = CAP // CHUNK
GU_TILE = 1024
ORDER = (1, 3, 2)


def slot_kernel(tok_in, ids_in, fixed_in, wg, wu, wd, out,
                tok, ids, fixed, small_sem, pk, xb, hid, yown, ysend, zin, psend, precv, rsend, ret, pick, vg, vu, vd,
                g_sem, u_sem, d_sem, z_ssem, z_rsem, y_ssem, y_rsem, b_ssem, b_rsem,
                k_ssem, k_rsem, p_ssem, p_rsem, r_ssem, r_rsem):
    rows, half = tok.shape
    ff = hid.shape[1]
    block = EXPERTS * CHUNK
    me = lax.axis_index("expert")
    core = lax.axis_index("tensor")
    other = 1 - core
    z, y = me // 2, me % 2

    def flip(r):
        hi = z // 2 if r < 2 else 1 - z // 2
        lo = z % 2 if r % 2 == 0 else 1 - z % 2
        return 2 * hi + lo

    sibling = {"tensor": other}
    across = {"expert": 2 * z + 1 - y}
    along = {r: {"expert": 2 * flip(r) + y} for r in range(1, EXPERTS)}

    barrier = pltpu.get_barrier_semaphore()
    for target in (*along.values(), across, sibling):
        pl.semaphore_signal(barrier, inc=1, device_id=target, device_id_type=pl.DeviceIdType.MESH)

    small = [pltpu.make_async_copy(src, dst, small_sem.at[i]) for i, (src, dst) in
             enumerate(((ids_in, ids), (tok_in, tok), (fixed_in, fixed)))]
    for copy in small:
        copy.start()

    tile = min(GU_TILE, ff)
    tiles = ff // tile

    def weight_copies(j):
        cols = pl.ds(j * tile, tile)
        return (pltpu.make_async_copy(wg.at[0, :, cols], vg.at[:, cols], g_sem.at[j]),
                pltpu.make_async_copy(wu.at[0, :, cols], vu.at[:, cols], u_sem.at[j]))

    def down_copy(which):
        cols = pl.ds(pl.multiple_of(which * half, half), half)
        return pltpu.make_async_copy(wd.at[0, :, cols], vd.at[:, cols], d_sem.at[which])

    for j in range(tiles):
        for copy in weight_copies(j):
            copy.start()
    down_copy(other).start()
    down_copy(core).start()

    small[0].wait()
    i0, i1 = ids[0:1, :], ids[1:2, :]
    match = [jnp.where((i0 == flip(r)) | (i1 == flip(r)), 1.0, 0.0) for r in range(EXPERTS)]
    before = (lax.broadcasted_iota(jnp.int32, (rows, rows), 0)
              < lax.broadcasted_iota(jnp.int32, (rows, rows), 1))
    stacked = jnp.concatenate(match + [jnp.zeros((8 - EXPERTS, rows), F32)], axis=0)
    pos = jnp.dot(stacked.astype(BF16), jnp.where(before, 1.0, 0.0).astype(BF16),
                  preferred_element_type=F32)
    slot = [jnp.where(match[r] > 0.0, pos[r:r + 1, :], -1.0) for r in range(EXPERTS)]
    number = lax.broadcasted_iota(jnp.int32, (CAP, rows), 0).astype(F32)
    small[1].wait()
    for r in range(EXPERTS):
        chosen = jnp.where(slot[r] == number, 1.0, 0.0).astype(BF16)
        pk[r] = jnp.dot(chosen, tok[...], preferred_element_type=F32).astype(BF16)
    pl.semaphore_wait(barrier, EXPERTS + 1)

    def remote(src, dst, ssem, rsem, target):
        return pltpu.make_async_remote_copy(
            src_ref=src, dst_ref=dst, send_sem=ssem, recv_sem=rsem,
            device_id=target, device_id_type=pl.DeviceIdType.MESH)

    def slots(c):
        return pl.ds(c * CHUNK, CHUNK)

    def unit(q, r):
        return pl.ds(q * block + r * CHUNK, CHUNK)

    def z_copy(r, c):
        return remote(pk.at[r, slots(c)], xb.at[c, core, unit(0, r)],
                      z_ssem.at[r, c], z_rsem.at[r, c], along[r])

    def y_copy(r, c):
        src = pk.at[0, slots(c)] if r == 0 else xb.at[c, core, unit(0, r)]
        return remote(src, xb.at[c, core, unit(1, r)], y_ssem.at[r, c], y_rsem.at[r, c], across)

    def b_copy(q, c):
        place = xb.at[c, core, pl.ds(q * block, block)]
        return remote(place, place, b_ssem.at[q, c], b_rsem.at[q, c], sibling)

    def k_copy(c):
        return remote(ysend.at[c], zin.at[c], k_ssem.at[c], k_rsem.at[c], sibling)

    def p_copy(r, c):
        return remote(psend.at[c, unit(0, r)], precv.at[c, unit(0, r)],
                      p_ssem.at[r, c], p_rsem.at[r, c], across)

    def r_copy(r, c):
        dst = ret.at[pl.ds(r * CAP + c * CHUNK, CHUNK)]
        return remote(rsend.at[c, unit(0, r)], dst, r_ssem.at[r, c], r_rsem.at[r, c], along[r])

    for c in range(PARTS):
        for r in ORDER:
            z_copy(r, c).start()
        y_copy(0, c).start()

    for c in range(PARTS):
        xb[c, core, 0:CHUNK, :] = pk[0, c * CHUNK:(c + 1) * CHUNK, :]

    small[2].wait()
    f0, f1 = fixed[0:1, :].astype(F32), fixed[1:2, :].astype(F32)
    s0, s1 = f0 / (f0 + f1), f1 / (f0 + f1)
    diag = (lax.broadcasted_iota(jnp.int32, (rows, rows), 0)
            == lax.broadcasted_iota(jnp.int32, (rows, rows), 1))

    def column(row):
        return jnp.sum(jnp.where(diag, row, 0.0), axis=1, keepdims=True)

    lane = lax.broadcasted_iota(jnp.int32, (rows, EXPERTS * CAP), 1).astype(F32)
    weigh = jnp.zeros((rows, EXPERTS * CAP), F32)
    for r in range(EXPERTS):
        e = flip(r)
        share = jnp.where(i0 == e, s0, 0.0) + jnp.where(i1 == e, s1, 0.0)
        place = column(jnp.where(match[r] > 0.0, pos[r:r + 1, :] + float(r * CAP), -1.0))
        weigh = weigh + jnp.where(place == lane, column(share), 0.0)
    high = weigh.astype(BF16)
    pick[0:rows, :] = high
    pick[rows:2 * rows, :] = (weigh - high.astype(F32)).astype(BF16)

    def relay(c):
        for r in ORDER:
            z_copy(r, c).wait_recv()
            y_copy(r, c).start()
        b_copy(0, c).start()

    def spread(c):
        for r in range(EXPERTS):
            y_copy(r, c).wait_recv()
        b_copy(1, c).start()

    def to_partner(c):
        k_copy(c).wait_recv()
        for r in (3, 2, 1, 0):
            piece = pl.ds(block + r * CHUNK, CHUNK)
            psend[c, unit(0, r), :] = (yown[c, piece, :] + zin[c, piece, :].astype(F32)).astype(BF16)
            p_copy(r, c).start()

    def to_origin(c, r):
        p_copy(r, c).wait_recv()
        piece = unit(0, r)
        total = (yown[c, piece, :] + zin[c, piece, :].astype(F32)
                 + precv[c, piece, :].astype(F32)).astype(BF16)
        if r == 0:
            ret[slots(c), :] = total
        else:
            rsend[c, piece, :] = total
            r_copy(r, c).start()

    relay(0)
    spread(0)
    relay(1)

    def down(c, which):
        if c == 0:
            down_copy(which).wait()
        cols = pl.ds(pl.multiple_of(which * half, half), half)
        return jnp.dot(hid[...], vd[:, cols], preferred_element_type=F32)

    for c in range(PARTS):
        b_copy(0, c).wait_recv()
        b_copy(1, c).wait_recv()
        if c > 1:
            to_origin(c - 2, 3)
        if c > 0:
            to_partner(c - 1)
        for j in range(tiles):
            if c == 0:
                for copy in weight_copies(j):
                    copy.wait()
            cols = pl.ds(j * tile, tile)
            a, b = xb[c, 0], xb[c, 1]
            g = (jnp.dot(a, vg[0:half, cols], preferred_element_type=F32)
                 + jnp.dot(b, vg[half:2 * half, cols], preferred_element_type=F32))
            u = (jnp.dot(a, vu[0:half, cols], preferred_element_type=F32)
                 + jnp.dot(b, vu[half:2 * half, cols], preferred_element_type=F32))
            hid[:, cols] = (g / (1.0 + jnp.exp(-g)) * u).astype(BF16)
            if j == 0 and c > 1:
                to_origin(c - 2, 2)
        if c < PARTS - 2:
            relay(c + 2)
        if c > 1:
            to_origin(c - 2, 1)
            to_origin(c - 2, 0)
        ysend[c] = down(c, other).astype(BF16)
        k_copy(c).start()
        if c < PARTS - 1:
            spread(c + 1)
        yown[c] = down(c, core)

    to_origin(PARTS - 2, 3)
    to_partner(PARTS - 1)
    for r in (2, 1, 0):
        to_origin(PARTS - 2, r)
    for r in (3, 2, 1, 0):
        to_origin(PARTS - 1, r)

    for c in range(PARTS):
        for r in (1, 2, 3):
            r_copy(r, c).wait_recv()
    mixed = jnp.dot(pick[...], ret[...], preferred_element_type=F32)
    out[...] = (mixed[0:rows] + mixed[rows:2 * rows]).astype(BF16)

    for c in range(PARTS):
        for r in range(EXPERTS):
            if r:
                z_copy(r, c).wait_send()
                r_copy(r, c).wait_send()
            y_copy(r, c).wait_send()
            p_copy(r, c).wait_send()
        for q in range(2):
            b_copy(q, c).wait_send()
        k_copy(c).wait_send()


def slot_per_device(tokens, expert_ids, gate_fixed, gate_weight, up_weight, down_weight):
    rows, half = tokens.shape
    ff = gate_weight.shape[2]
    tiles = ff // min(GU_TILE, ff)
    many = 2 * EXPERTS * CHUNK
    dma = pltpu.SemaphoreType.DMA
    vmem = pl.BlockSpec(memory_space=pltpu.VMEM)
    hbm = pl.BlockSpec(memory_space=pl.ANY)
    return pl.pallas_call(
        slot_kernel,
        out_shape=pltpu.VMEM((rows, half), BF16),
        in_specs=[hbm] * 6,
        out_specs=vmem,
        scratch_shapes=[
            pltpu.VMEM((rows, half), BF16),
            pltpu.VMEM((2, rows), jnp.int32),
            pltpu.VMEM((2, rows), jnp.int32),
            dma((3,)),
            pltpu.VMEM((EXPERTS, CAP, half), BF16),
            pltpu.VMEM((PARTS, 2, many, half), BF16),
            pltpu.VMEM((many, ff), BF16),
            pltpu.VMEM((PARTS, many, half), F32),
            pltpu.VMEM((PARTS, many, half), BF16),
            pltpu.VMEM((PARTS, many, half), BF16),
            pltpu.VMEM((PARTS, many // 2, half), BF16),
            pltpu.VMEM((PARTS, many // 2, half), BF16),
            pltpu.VMEM((PARTS, many // 2, half), BF16),
            pltpu.VMEM((EXPERTS * CAP, half), BF16),
            pltpu.VMEM((2 * rows, EXPERTS * CAP), BF16),
            pltpu.VMEM((2 * half, ff), BF16),
            pltpu.VMEM((2 * half, ff), BF16),
            pltpu.VMEM((ff, 2 * half), BF16),
            dma((tiles,)), dma((tiles,)), dma((2,)),
            dma((EXPERTS, PARTS)), dma((EXPERTS, PARTS)),
            dma((EXPERTS, PARTS)), dma((EXPERTS, PARTS)),
            dma((2, PARTS)), dma((2, PARTS)),
            dma((PARTS,)), dma((PARTS,)),
            dma((EXPERTS, PARTS)), dma((EXPERTS, PARTS)),
            dma((EXPERTS, PARTS)), dma((EXPERTS, PARTS)),
        ],
        compiler_params=pltpu.CompilerParams(
            collective_id=0, has_side_effects=True, vmem_limit_bytes=60 * 1024 * 1024),
    )(tokens, expert_ids.T, gate_fixed.T, gate_weight, up_weight, down_weight)


def solution(mesh):
    placed = (
        P(("group", "expert"), "tensor"),
        P(("group", "expert"), None),
        P(("group", "expert"), None),
        P("expert", None, "tensor"),
        P("expert", None, "tensor"),
        P("expert", "tensor", None),
    )
    return jax.shard_map(
        slot_per_device if mesh.shape["expert"] == 2 * EXPERTS else ring_per_device,
        mesh=mesh,
        in_specs=placed,
        out_specs=P(("group", "expert"), "tensor"),
        check_vma=False,
    )
```

```python
import functools

import jax
import jax.numpy as jnp
from jax import lax
from jax.experimental import pallas as pl
from jax.experimental.pallas import tpu as pltpu
from jax.sharding import PartitionSpec as P

EXPERTS = 4
TILE = 1024
DOWN_TILE = 768
F32 = jnp.float32
BF16 = jnp.bfloat16


def ring_kernel(n, tok, ids, fixed, wg, wu, wd, out,
           xb, wt, hid, yown, ysend, zin, psend, precv, vg, vu, vd,
           g_sem, u_sem, d_sem, x_ssem, x_rsem, w_ssem, w_rsem, b_ssem, b_rsem,
           z_ssem, z_rsem, p_ssem, p_rsem):
    h = n // 2
    rows, half = tok.shape
    part = rows // 2
    me = lax.axis_index("expert")
    core = lax.axis_index("tensor")
    other = 1 - core
    expert = me // (n // EXPERTS)
    odd = me % 2
    pos = (1 - odd) * (me // 2) + odd * (n - 1 - me // 2)

    def at_pos(p):
        p = (p + n) % n
        back = p // h
        return (1 - back) * (2 * p) + back * (2 * (n - 1 - p) + 1)

    onward = ({"expert": at_pos(pos + 1)}, {"expert": at_pos(pos - 1)})
    sibling = {"tensor": other}

    ff = hid.shape[1]
    tile = min(TILE, ff)
    j_hidden = ff // tile
    j_half = half // DOWN_TILE

    def hidden_cols(j):
        return pl.ds(pl.multiple_of(j * tile, tile), tile)

    def out_cols(j):
        return pl.ds(pl.multiple_of(j * DOWN_TILE, DOWN_TILE), DOWN_TILE)

    def weight_copies(j):
        cols = hidden_cols(j)
        return (pltpu.make_async_copy(wg.at[0, :, cols], vg.at[:, cols], g_sem.at[j]),
                pltpu.make_async_copy(wu.at[0, :, cols], vu.at[:, cols], u_sem.at[j]))

    def down_copy(j):
        cols = out_cols(j)
        return pltpu.make_async_copy(wd.at[0, :, cols], vd.at[:, cols], d_sem.at[j])

    @pl.loop(0, j_hidden)
    def _(j):
        for copy in weight_copies(j):
            copy.start()

    @pl.loop(0, 2 * j_half)
    def _(j):
        down_copy(j).start()

    barrier = pltpu.get_barrier_semaphore()
    for target in onward + (sibling,):
        pl.semaphore_signal(barrier, inc=1, device_id=target, device_id_type=pl.DeviceIdType.MESH)

    diag = (lax.broadcasted_iota(jnp.int32, (rows, 128), 0)
            == lax.broadcasted_iota(jnp.int32, (rows, 128), 1))
    f0 = fixed[:, 0:1].astype(F32)
    f1 = fixed[:, 1:2].astype(F32)
    total = f0 + f1
    s0, s1 = f0 / total, f1 / total
    i0, i1 = ids[:, 0:1], ids[:, 1:2]
    wt[0, 0] = jnp.zeros((8, 128), F32)
    for e in range(EXPERTS):
        col = jnp.where(i0 == e, s0, 0.0) + jnp.where(i1 == e, s1, 0.0)
        wt[0, 0, e:e + 1, :] = jnp.sum(jnp.where(diag, col, 0.0), axis=0, keepdims=True)
    xb[0, core, 0:rows, :] = tok[...]
    pl.semaphore_wait(barrier, 3)

    def remote(src, dst, ssem, rsem, target):
        return pltpu.make_async_remote_copy(
            src_ref=src, dst_ref=dst, send_sem=ssem, recv_sem=rsem,
            device_id=target, device_id_type=pl.DeviceIdType.MESH)

    def x_copy(d, s, q):
        piece = pl.ds(d * rows + q * part, part)
        return remote(xb.at[s - 1, core, piece], xb.at[s, core, piece],
                      x_ssem.at[d, s, q], x_rsem.at[d, s, q], onward[d])

    def x_first(d, q):
        return remote(xb.at[0, core, pl.ds(q * part, part)],
                      xb.at[1, core, pl.ds(d * rows + q * part, part)],
                      x_ssem.at[d, 1, q], x_rsem.at[d, 1, q], onward[d])

    def x_last(d):
        return remote(xb.at[h - 1, core, pl.ds(d * rows + d * part, part)],
                      xb.at[0, core, pl.ds(rows + d * part, part)],
                      x_ssem.at[d, h, d], x_rsem.at[d, h, d], onward[d])

    def w_copy(d, s):
        return remote(wt.at[s - 1, d], wt.at[s, d], w_ssem.at[d, s], w_rsem.at[d, s], onward[d])

    def w_first(d):
        return remote(wt.at[0, 0], wt.at[1, d], w_ssem.at[d, 1], w_rsem.at[d, 1], onward[d])

    def w_last():
        return remote(wt.at[h - 1, 0], wt.at[0, 1], w_ssem.at[0, h], w_rsem.at[0, h], onward[0])

    def b_copy(d, s):
        place = xb.at[s, core, pl.ds(d * rows, rows)]
        return remote(place, place, b_ssem.at[d, s], b_rsem.at[d, s], sibling)

    def z_copy(s):
        return remote(ysend.at[s], zin.at[s], z_ssem.at[s], z_rsem.at[s], sibling)

    for d in range(2):
        w_first(d).start()
    for q in range(2):
        for d in range(2):
            x_first(d, d if q == 0 else 1 - d).start()
    b_copy(0, 0).start()

    def compute(s, first):
        @pl.loop(0, j_hidden)
        def _(j):
            cols = hidden_cols(j)

            @pl.when(first)
            def _():
                for copy in weight_copies(j):
                    copy.wait()

            a, b = xb[s, 0], xb[s, 1]
            g = (jnp.dot(a, vg[0:half, cols], preferred_element_type=F32)
                 + jnp.dot(b, vg[half:2 * half, cols], preferred_element_type=F32))
            u = (jnp.dot(a, vu[0:half, cols], preferred_element_type=F32)
                 + jnp.dot(b, vu[half:2 * half, cols], preferred_element_type=F32))
            hid[:, cols] = (g / (1.0 + jnp.exp(-g)) * u).astype(BF16)

        share = jnp.concatenate(
            [jnp.sum(jnp.where(diag, wt[s, d, pl.ds(expert, 1), :], 0.0), axis=1, keepdims=True)
             for d in range(2)], axis=0)

        def down(j, which):
            cols = pl.ds(pl.multiple_of(which * half + j * DOWN_TILE, DOWN_TILE), DOWN_TILE)

            @pl.when(first)
            def _():
                down_copy(which * j_half + j).wait()

            return jnp.dot(hid[...], vd[:, cols], preferred_element_type=F32) * share

        @pl.loop(0, j_half)
        def _(j):
            ysend[s, :, out_cols(j)] = down(j, other).astype(BF16)

        z_copy(s).start()

        @pl.loop(0, j_half)
        def _(j):
            yown[s, :, out_cols(j)] = down(j, core)

    def step(s, carry):
        for turn in range(2):
            for d in range(2):
                q = d if turn == 0 else 1 - d
                x_copy(d, s, q).wait_recv()

                @pl.when(s < h - 1)
                def _():
                    x_copy(d, s + 1, q).start()

                if turn == 0:
                    @pl.when(s == h - 1)
                    def _():
                        x_last(d).start()

        for d in range(2):
            w_copy(d, s).wait_recv()

        @pl.when(s < h - 1)
        def _():
            for d in range(2):
                w_copy(d, s + 1).start()

        @pl.when(s == h - 1)
        def _():
            w_last().start()

        for d in range(2):
            b_copy(d, s).start()
        for d in range(2):
            b_copy(d, s).wait_recv()
        compute(s, s == 1)
        return carry

    lax.fori_loop(1, h, step, 0)
    for d in range(2):
        x_last(d).wait_recv()
    w_last().wait_recv()
    b_copy(1, 0).start()
    b_copy(0, 0).wait_recv()
    b_copy(1, 0).wait_recv()
    compute(0, False)

    def p_copy(d, k, q):
        piece = pl.ds(q * part, part)
        return remote(psend.at[d, k, piece], precv.at[d, k, piece],
                      p_ssem.at[d, k, q], p_rsem.at[d, k, q], onward[d])

    z_copy(0).wait_recv()
    for k in range(h, 0, -1):
        slot = k % h
        if k < h:
            z_copy(k).wait_recv()
        for turn in range(2):
            for d in range(2):
                q = (1 - d) if turn == 0 else d
                if k == h and q != d:
                    continue
                base = (rows if k == h or d == 0 else 0) + q * part
                total = yown[slot, base:base + part, :] + zin[slot, base:base + part, :].astype(F32)
                if k < h - 1 or (k == h - 1 and q == d):
                    p_copy(d, k, q).wait_recv()
                    total = total + precv[d, k, q * part:(q + 1) * part, :].astype(F32)
                psend[d, k - 1, q * part:(q + 1) * part, :] = total.astype(BF16)
                p_copy(d, k - 1, q).start()
    for q in (0, 1):
        total = yown[0, q * part:(q + 1) * part, :] + zin[0, q * part:(q + 1) * part, :].astype(F32)
        for d in range(2):
            p_copy(d, 0, q).wait_recv()
            total = total + precv[d, 0, q * part:(q + 1) * part, :].astype(F32)
        out[q * part:(q + 1) * part, :] = total.astype(BF16)

    for d in range(2):
        for q in range(2):
            x_first(d, q).wait_send()
        w_first(d).wait_send()
        x_last(d).wait_send()
        for k in range(h):
            for q in range(2):
                if k < h - 1 or q == d:
                    p_copy(d, k, q).wait_send()
    w_last().wait_send()

    def drain(s, carry):
        for d in range(2):
            for q in range(2):
                x_copy(d, s, q).wait_send()
            w_copy(d, s).wait_send()
        return carry

    lax.fori_loop(2, h, drain, 0)

    def drain_sibling(s, carry):
        for d in range(2):
            b_copy(d, s).wait_send()
        z_copy(s).wait_send()
        return carry

    lax.fori_loop(0, h, drain_sibling, 0)


def ring_per_device(tokens, expert_ids, gate_fixed, gate_weight, up_weight, down_weight):
    n = lax.axis_size("expert")
    h = n // 2
    rows, half = tokens.shape
    ff = gate_weight.shape[2]
    dma = pltpu.SemaphoreType.DMA
    vmem = pl.BlockSpec(memory_space=pltpu.VMEM)
    hbm = pl.BlockSpec(memory_space=pl.ANY)
    return pl.pallas_call(
        functools.partial(ring_kernel, n),
        out_shape=jax.ShapeDtypeStruct((rows, half), BF16),
        in_specs=[vmem, vmem, vmem, hbm, hbm, hbm],
        out_specs=vmem,
        scratch_shapes=[
            pltpu.VMEM((h, 2, 2 * rows, half), BF16),
            pltpu.VMEM((h, 2, 8, 128), F32),
            pltpu.VMEM((2 * rows, ff), BF16),
            pltpu.VMEM((h, 2 * rows, half), F32),
            pltpu.VMEM((h, 2 * rows, half), BF16),
            pltpu.VMEM((h, 2 * rows, half), BF16),
            pltpu.VMEM((2, h, rows, half), BF16),
            pltpu.VMEM((2, h, rows, half), BF16),
            pltpu.VMEM((2 * half, ff), BF16),
            pltpu.VMEM((2 * half, ff), BF16),
            pltpu.VMEM((ff, 2 * half), BF16),
            dma((ff // min(TILE, ff),)), dma((ff // min(TILE, ff),)), dma((2 * half // DOWN_TILE,)),
            dma((2, h + 1, 2)), dma((2, h + 1, 2)),
            dma((2, h + 1)), dma((2, h + 1)),
            dma((2, h)), dma((2, h)),
            dma((h,)), dma((h,)),
            dma((2, h, 2)), dma((2, h, 2)),
        ],
        compiler_params=pltpu.CompilerParams(
            collective_id=0, has_side_effects=True, vmem_limit_bytes=60 * 1024 * 1024),
    )(tokens, expert_ids, gate_fixed, gate_weight, up_weight, down_weight)


CAP = 48
CHUNK = 16
PARTS = CAP // CHUNK
GU_TILE = 1024
ORDER = (1, 3, 2)


def slot_kernel(tok_in, ids_in, fixed_in, wg, wu, wd, out,
                tok, ids, fixed, small_sem, pk, xb, hid, yown, ysend, zin, psend, precv, rsend, ret, pick, vg, vu, vd,
                g_sem, u_sem, d_sem, z_ssem, z_rsem, y_ssem, y_rsem, b_ssem, b_rsem,
                k_ssem, k_rsem, p_ssem, p_rsem, r_ssem, r_rsem):
    rows, half = tok.shape
    ff = hid.shape[1]
    block = EXPERTS * CHUNK
    me = lax.axis_index("expert")
    core = lax.axis_index("tensor")
    other = 1 - core
    z, y = me // 2, me % 2

    def flip(r):
        hi = z // 2 if r < 2 else 1 - z // 2
        lo = z % 2 if r % 2 == 0 else 1 - z % 2
        return 2 * hi + lo

    sibling = {"tensor": other}
    across = {"expert": 2 * z + 1 - y}
    along = {r: {"expert": 2 * flip(r) + y} for r in range(1, EXPERTS)}

    barrier = pltpu.get_barrier_semaphore()
    for target in (*along.values(), across, sibling):
        pl.semaphore_signal(barrier, inc=1, device_id=target, device_id_type=pl.DeviceIdType.MESH)

    small = [pltpu.make_async_copy(src, dst, small_sem.at[i]) for i, (src, dst) in
             enumerate(((ids_in, ids), (tok_in, tok), (fixed_in, fixed)))]
    for copy in small:
        copy.start()

    tile = min(GU_TILE, ff)
    tiles = ff // tile

    def weight_copies(j):
        cols = pl.ds(j * tile, tile)
        return (pltpu.make_async_copy(wg.at[0, :, cols], vg.at[:, cols], g_sem.at[j]),
                pltpu.make_async_copy(wu.at[0, :, cols], vu.at[:, cols], u_sem.at[j]))

    def down_copy(which):
        cols = pl.ds(pl.multiple_of(which * half, half), half)
        return pltpu.make_async_copy(wd.at[0, :, cols], vd.at[:, cols], d_sem.at[which])

    for j in range(tiles):
        for copy in weight_copies(j):
            copy.start()
    down_copy(other).start()
    down_copy(core).start()

    small[0].wait()
    i0, i1 = ids[0:1, :], ids[1:2, :]
    match = [jnp.where((i0 == flip(r)) | (i1 == flip(r)), 1.0, 0.0) for r in range(EXPERTS)]
    before = (lax.broadcasted_iota(jnp.int32, (rows, rows), 0)
              < lax.broadcasted_iota(jnp.int32, (rows, rows), 1))
    stacked = jnp.concatenate(match + [jnp.zeros((8 - EXPERTS, rows), F32)], axis=0)
    pos = jnp.dot(stacked.astype(BF16), jnp.where(before, 1.0, 0.0).astype(BF16),
                  preferred_element_type=F32)
    slot = [jnp.where(match[r] > 0.0, pos[r:r + 1, :], -1.0) for r in range(EXPERTS)]
    number = lax.broadcasted_iota(jnp.int32, (CAP, rows), 0).astype(F32)
    small[1].wait()
    for r in range(EXPERTS):
        chosen = jnp.where(slot[r] == number, 1.0, 0.0).astype(BF16)
        pk[r] = jnp.dot(chosen, tok[...], preferred_element_type=F32).astype(BF16)
    pl.semaphore_wait(barrier, EXPERTS + 1)

    def remote(src, dst, ssem, rsem, target):
        return pltpu.make_async_remote_copy(
            src_ref=src, dst_ref=dst, send_sem=ssem, recv_sem=rsem,
            device_id=target, device_id_type=pl.DeviceIdType.MESH)

    def slots(c):
        return pl.ds(c * CHUNK, CHUNK)

    def unit(q, r):
        return pl.ds(q * block + r * CHUNK, CHUNK)

    def z_copy(r, c):
        return remote(pk.at[r, slots(c)], xb.at[c, core, unit(0, r)],
                      z_ssem.at[r, c], z_rsem.at[r, c], along[r])

    def y_copy(r, c):
        src = pk.at[0, slots(c)] if r == 0 else xb.at[c, core, unit(0, r)]
        return remote(src, xb.at[c, core, unit(1, r)], y_ssem.at[r, c], y_rsem.at[r, c], across)

    def b_copy(q, c):
        place = xb.at[c, core, pl.ds(q * block, block)]
        return remote(place, place, b_ssem.at[q, c], b_rsem.at[q, c], sibling)

    def k_copy(c):
        return remote(ysend.at[c], zin.at[c], k_ssem.at[c], k_rsem.at[c], sibling)

    def p_copy(r, c):
        return remote(psend.at[c, unit(0, r)], precv.at[c, unit(0, r)],
                      p_ssem.at[r, c], p_rsem.at[r, c], across)

    def r_copy(r, c):
        dst = ret.at[pl.ds(r * CAP + c * CHUNK, CHUNK)]
        return remote(rsend.at[c, unit(0, r)], dst, r_ssem.at[r, c], r_rsem.at[r, c], along[r])

    for c in range(PARTS):
        for r in ORDER:
            z_copy(r, c).start()
        y_copy(0, c).start()

    for c in range(PARTS):
        xb[c, core, 0:CHUNK, :] = pk[0, c * CHUNK:(c + 1) * CHUNK, :]

    small[2].wait()
    f0, f1 = fixed[0:1, :].astype(F32), fixed[1:2, :].astype(F32)
    s0, s1 = f0 / (f0 + f1), f1 / (f0 + f1)
    diag = (lax.broadcasted_iota(jnp.int32, (rows, rows), 0)
            == lax.broadcasted_iota(jnp.int32, (rows, rows), 1))

    def column(row):
        return jnp.sum(jnp.where(diag, row, 0.0), axis=1, keepdims=True)

    lane = lax.broadcasted_iota(jnp.int32, (rows, EXPERTS * CAP), 1).astype(F32)
    weigh = jnp.zeros((rows, EXPERTS * CAP), F32)
    for r in range(EXPERTS):
        e = flip(r)
        share = jnp.where(i0 == e, s0, 0.0) + jnp.where(i1 == e, s1, 0.0)
        place = column(jnp.where(match[r] > 0.0, pos[r:r + 1, :] + float(r * CAP), -1.0))
        weigh = weigh + jnp.where(place == lane, column(share), 0.0)
    high = weigh.astype(BF16)
    pick[0:rows, :] = high
    pick[rows:2 * rows, :] = (weigh - high.astype(F32)).astype(BF16)

    def relay(c):
        for r in ORDER:
            z_copy(r, c).wait_recv()
            y_copy(r, c).start()
        b_copy(0, c).start()

    def spread(c):
        for r in range(EXPERTS):
            y_copy(r, c).wait_recv()
        b_copy(1, c).start()

    def to_partner(c):
        k_copy(c).wait_recv()
        for r in (3, 2, 1, 0):
            piece = pl.ds(block + r * CHUNK, CHUNK)
            psend[c, unit(0, r), :] = (yown[c, piece, :] + zin[c, piece, :].astype(F32)).astype(BF16)
            p_copy(r, c).start()

    def to_origin(c, r):
        p_copy(r, c).wait_recv()
        piece = unit(0, r)
        total = (yown[c, piece, :] + zin[c, piece, :].astype(F32)
                 + precv[c, piece, :].astype(F32)).astype(BF16)
        if r == 0:
            ret[slots(c), :] = total
        else:
            rsend[c, piece, :] = total
            r_copy(r, c).start()

    relay(0)
    spread(0)
    relay(1)

    def down(c, which):
        if c == 0:
            down_copy(which).wait()
        cols = pl.ds(pl.multiple_of(which * half, half), half)
        return jnp.dot(hid[...], vd[:, cols], preferred_element_type=F32)

    for c in range(PARTS):
        b_copy(0, c).wait_recv()
        b_copy(1, c).wait_recv()
        if c > 1:
            to_origin(c - 2, 2)
        if c > 0:
            to_partner(c - 1)
        for j in range(tiles):
            if c == 0:
                for copy in weight_copies(j):
                    copy.wait()
            cols = pl.ds(j * tile, tile)
            a, b = xb[c, 0], xb[c, 1]
            g = (jnp.dot(a, vg[0:half, cols], preferred_element_type=F32)
                 + jnp.dot(b, vg[half:2 * half, cols], preferred_element_type=F32))
            u = (jnp.dot(a, vu[0:half, cols], preferred_element_type=F32)
                 + jnp.dot(b, vu[half:2 * half, cols], preferred_element_type=F32))
            hid[:, cols] = (g / (1.0 + jnp.exp(-g)) * u).astype(BF16)
            if j == 0 and c > 1:
                to_origin(c - 2, 1)
                to_origin(c - 2, 0)
        if c < PARTS - 2:
            relay(c + 2)
        ysend[c] = down(c, other).astype(BF16)
        k_copy(c).start()
        if c < PARTS - 1:
            spread(c + 1)
        if c > 0:
            to_origin(c - 1, 3)
        yown[c] = down(c, core)

    to_origin(PARTS - 2, 2)
    to_partner(PARTS - 1)
    for r in (1, 0):
        to_origin(PARTS - 2, r)
    for c in range(PARTS):
        for r in range(EXPERTS):
            if r:
                z_copy(r, c).wait_send()
            y_copy(r, c).wait_send()
        for q in range(2):
            b_copy(q, c).wait_send()
        k_copy(c).wait_send()
    for r in (3, 2, 1, 0):
        to_origin(PARTS - 1, r)
    for c in range(PARTS):
        for r in range(EXPERTS):
            p_copy(r, c).wait_send()
            if r:
                r_copy(r, c).wait_send()

    for c in range(PARTS):
        for r in (1, 2, 3):
            r_copy(r, c).wait_recv()
    mixed = jnp.dot(pick[...], ret[...], preferred_element_type=F32)
    out[...] = (mixed[0:rows] + mixed[rows:2 * rows]).astype(BF16)


def slot_per_device(tokens, expert_ids, gate_fixed, gate_weight, up_weight, down_weight):
    rows, half = tokens.shape
    ff = gate_weight.shape[2]
    tiles = ff // min(GU_TILE, ff)
    many = 2 * EXPERTS * CHUNK
    dma = pltpu.SemaphoreType.DMA
    vmem = pl.BlockSpec(memory_space=pltpu.VMEM)
    hbm = pl.BlockSpec(memory_space=pl.ANY)
    return pl.pallas_call(
        slot_kernel,
        out_shape=pltpu.VMEM((rows, half), BF16),
        in_specs=[hbm] * 6,
        out_specs=vmem,
        scratch_shapes=[
            pltpu.VMEM((rows, half), BF16),
            pltpu.VMEM((2, rows), jnp.int32),
            pltpu.VMEM((2, rows), jnp.int32),
            dma((3,)),
            pltpu.VMEM((EXPERTS, CAP, half), BF16),
            pltpu.VMEM((PARTS, 2, many, half), BF16),
            pltpu.VMEM((many, ff), BF16),
            pltpu.VMEM((PARTS, many, half), F32),
            pltpu.VMEM((PARTS, many, half), BF16),
            pltpu.VMEM((PARTS, many, half), BF16),
            pltpu.VMEM((PARTS, many // 2, half), BF16),
            pltpu.VMEM((PARTS, many // 2, half), BF16),
            pltpu.VMEM((PARTS, many // 2, half), BF16),
            pltpu.VMEM((EXPERTS * CAP, half), BF16),
            pltpu.VMEM((2 * rows, EXPERTS * CAP), BF16),
            pltpu.VMEM((2 * half, ff), BF16),
            pltpu.VMEM((2 * half, ff), BF16),
            pltpu.VMEM((ff, 2 * half), BF16),
            dma((tiles,)), dma((tiles,)), dma((2,)),
            dma((EXPERTS, PARTS)), dma((EXPERTS, PARTS)),
            dma((EXPERTS, PARTS)), dma((EXPERTS, PARTS)),
            dma((2, PARTS)), dma((2, PARTS)),
            dma((PARTS,)), dma((PARTS,)),
            dma((EXPERTS, PARTS)), dma((EXPERTS, PARTS)),
            dma((EXPERTS, PARTS)), dma((EXPERTS, PARTS)),
        ],
        compiler_params=pltpu.CompilerParams(
            collective_id=0, has_side_effects=True, vmem_limit_bytes=60 * 1024 * 1024),
    )(tokens, expert_ids.T, gate_fixed.T, gate_weight, up_weight, down_weight)


def solution(mesh):
    placed = (
        P(("group", "expert"), "tensor"),
        P(("group", "expert"), None),
        P(("group", "expert"), None),
        P("expert", None, "tensor"),
        P("expert", None, "tensor"),
        P("expert", "tensor", None),
    )
    return jax.shard_map(
        slot_per_device if mesh.shape["expert"] == 2 * EXPERTS else ring_per_device,
        mesh=mesh,
        in_specs=placed,
        out_specs=P(("group", "expert"), "tensor"),
        check_vma=False,
    )
```

```python
import functools

import jax
import jax.numpy as jnp
from jax import lax
from jax.experimental import pallas as pl
from jax.experimental.pallas import tpu as pltpu
from jax.sharding import PartitionSpec as P

EXPERTS = 4
TILE = 1024
DOWN_TILE = 768
F32 = jnp.float32
BF16 = jnp.bfloat16


def ring_kernel(n, tok, ids, fixed, wg, wu, wd, out,
           xb, wt, hid, yown, ysend, zin, psend, precv, vg, vu, vd,
           g_sem, u_sem, d_sem, x_ssem, x_rsem, w_ssem, w_rsem, b_ssem, b_rsem,
           z_ssem, z_rsem, p_ssem, p_rsem):
    h = n // 2
    rows, half = tok.shape
    part = rows // 2
    me = lax.axis_index("expert")
    core = lax.axis_index("tensor")
    other = 1 - core
    expert = me // (n // EXPERTS)
    odd = me % 2
    pos = (1 - odd) * (me // 2) + odd * (n - 1 - me // 2)

    def at_pos(p):
        p = (p + n) % n
        back = p // h
        return (1 - back) * (2 * p) + back * (2 * (n - 1 - p) + 1)

    onward = ({"expert": at_pos(pos + 1)}, {"expert": at_pos(pos - 1)})
    sibling = {"tensor": other}

    ff = hid.shape[1]
    tile = min(TILE, ff)
    j_hidden = ff // tile
    j_half = half // DOWN_TILE

    def hidden_cols(j):
        return pl.ds(pl.multiple_of(j * tile, tile), tile)

    def out_cols(j):
        return pl.ds(pl.multiple_of(j * DOWN_TILE, DOWN_TILE), DOWN_TILE)

    def weight_copies(j):
        cols = hidden_cols(j)
        return (pltpu.make_async_copy(wg.at[0, :, cols], vg.at[:, cols], g_sem.at[j]),
                pltpu.make_async_copy(wu.at[0, :, cols], vu.at[:, cols], u_sem.at[j]))

    def down_copy(j):
        cols = out_cols(j)
        return pltpu.make_async_copy(wd.at[0, :, cols], vd.at[:, cols], d_sem.at[j])

    @pl.loop(0, j_hidden)
    def _(j):
        for copy in weight_copies(j):
            copy.start()

    @pl.loop(0, 2 * j_half)
    def _(j):
        down_copy(j).start()

    barrier = pltpu.get_barrier_semaphore()
    for target in onward + (sibling,):
        pl.semaphore_signal(barrier, inc=1, device_id=target, device_id_type=pl.DeviceIdType.MESH)

    diag = (lax.broadcasted_iota(jnp.int32, (rows, 128), 0)
            == lax.broadcasted_iota(jnp.int32, (rows, 128), 1))
    f0 = fixed[:, 0:1].astype(F32)
    f1 = fixed[:, 1:2].astype(F32)
    total = f0 + f1
    s0, s1 = f0 / total, f1 / total
    i0, i1 = ids[:, 0:1], ids[:, 1:2]
    wt[0, 0] = jnp.zeros((8, 128), F32)
    for e in range(EXPERTS):
        col = jnp.where(i0 == e, s0, 0.0) + jnp.where(i1 == e, s1, 0.0)
        wt[0, 0, e:e + 1, :] = jnp.sum(jnp.where(diag, col, 0.0), axis=0, keepdims=True)
    xb[0, core, 0:rows, :] = tok[...]
    pl.semaphore_wait(barrier, 3)

    def remote(src, dst, ssem, rsem, target):
        return pltpu.make_async_remote_copy(
            src_ref=src, dst_ref=dst, send_sem=ssem, recv_sem=rsem,
            device_id=target, device_id_type=pl.DeviceIdType.MESH)

    def x_copy(d, s, q):
        piece = pl.ds(d * rows + q * part, part)
        return remote(xb.at[s - 1, core, piece], xb.at[s, core, piece],
                      x_ssem.at[d, s, q], x_rsem.at[d, s, q], onward[d])

    def x_first(d, q):
        return remote(xb.at[0, core, pl.ds(q * part, part)],
                      xb.at[1, core, pl.ds(d * rows + q * part, part)],
                      x_ssem.at[d, 1, q], x_rsem.at[d, 1, q], onward[d])

    def x_last(d):
        return remote(xb.at[h - 1, core, pl.ds(d * rows + d * part, part)],
                      xb.at[0, core, pl.ds(rows + d * part, part)],
                      x_ssem.at[d, h, d], x_rsem.at[d, h, d], onward[d])

    def w_copy(d, s):
        return remote(wt.at[s - 1, d], wt.at[s, d], w_ssem.at[d, s], w_rsem.at[d, s], onward[d])

    def w_first(d):
        return remote(wt.at[0, 0], wt.at[1, d], w_ssem.at[d, 1], w_rsem.at[d, 1], onward[d])

    def w_last():
        return remote(wt.at[h - 1, 0], wt.at[0, 1], w_ssem.at[0, h], w_rsem.at[0, h], onward[0])

    def b_copy(d, s):
        place = xb.at[s, core, pl.ds(d * rows, rows)]
        return remote(place, place, b_ssem.at[d, s], b_rsem.at[d, s], sibling)

    def z_copy(s):
        return remote(ysend.at[s], zin.at[s], z_ssem.at[s], z_rsem.at[s], sibling)

    for d in range(2):
        w_first(d).start()
    for q in range(2):
        for d in range(2):
            x_first(d, d if q == 0 else 1 - d).start()
    b_copy(0, 0).start()

    def compute(s, first):
        @pl.loop(0, j_hidden)
        def _(j):
            cols = hidden_cols(j)

            @pl.when(first)
            def _():
                for copy in weight_copies(j):
                    copy.wait()

            a, b = xb[s, 0], xb[s, 1]
            g = (jnp.dot(a, vg[0:half, cols], preferred_element_type=F32)
                 + jnp.dot(b, vg[half:2 * half, cols], preferred_element_type=F32))
            u = (jnp.dot(a, vu[0:half, cols], preferred_element_type=F32)
                 + jnp.dot(b, vu[half:2 * half, cols], preferred_element_type=F32))
            hid[:, cols] = (g / (1.0 + jnp.exp(-g)) * u).astype(BF16)

        share = jnp.concatenate(
            [jnp.sum(jnp.where(diag, wt[s, d, pl.ds(expert, 1), :], 0.0), axis=1, keepdims=True)
             for d in range(2)], axis=0)

        def down(j, which):
            cols = pl.ds(pl.multiple_of(which * half + j * DOWN_TILE, DOWN_TILE), DOWN_TILE)

            @pl.when(first)
            def _():
                down_copy(which * j_half + j).wait()

            return jnp.dot(hid[...], vd[:, cols], preferred_element_type=F32) * share

        @pl.loop(0, j_half)
        def _(j):
            ysend[s, :, out_cols(j)] = down(j, other).astype(BF16)

        z_copy(s).start()

        @pl.loop(0, j_half)
        def _(j):
            yown[s, :, out_cols(j)] = down(j, core)

    def step(s, carry):
        for turn in range(2):
            for d in range(2):
                q = d if turn == 0 else 1 - d
                x_copy(d, s, q).wait_recv()

                @pl.when(s < h - 1)
                def _():
                    x_copy(d, s + 1, q).start()

                if turn == 0:
                    @pl.when(s == h - 1)
                    def _():
                        x_last(d).start()

        for d in range(2):
            w_copy(d, s).wait_recv()

        @pl.when(s < h - 1)
        def _():
            for d in range(2):
                w_copy(d, s + 1).start()

        @pl.when(s == h - 1)
        def _():
            w_last().start()

        for d in range(2):
            b_copy(d, s).start()
        for d in range(2):
            b_copy(d, s).wait_recv()
        compute(s, s == 1)
        return carry

    lax.fori_loop(1, h, step, 0)
    for d in range(2):
        x_last(d).wait_recv()
    w_last().wait_recv()
    b_copy(1, 0).start()
    b_copy(0, 0).wait_recv()
    b_copy(1, 0).wait_recv()
    compute(0, False)

    def p_copy(d, k, q):
        piece = pl.ds(q * part, part)
        return remote(psend.at[d, k, piece], precv.at[d, k, piece],
                      p_ssem.at[d, k, q], p_rsem.at[d, k, q], onward[d])

    z_copy(0).wait_recv()
    for k in range(h, 0, -1):
        slot = k % h
        if k < h:
            z_copy(k).wait_recv()
        for turn in range(2):
            for d in range(2):
                q = (1 - d) if turn == 0 else d
                if k == h and q != d:
                    continue
                base = (rows if k == h or d == 0 else 0) + q * part
                total = yown[slot, base:base + part, :] + zin[slot, base:base + part, :].astype(F32)
                if k < h - 1 or (k == h - 1 and q == d):
                    p_copy(d, k, q).wait_recv()
                    total = total + precv[d, k, q * part:(q + 1) * part, :].astype(F32)
                psend[d, k - 1, q * part:(q + 1) * part, :] = total.astype(BF16)
                p_copy(d, k - 1, q).start()
    for q in (0, 1):
        total = yown[0, q * part:(q + 1) * part, :] + zin[0, q * part:(q + 1) * part, :].astype(F32)
        for d in range(2):
            p_copy(d, 0, q).wait_recv()
            total = total + precv[d, 0, q * part:(q + 1) * part, :].astype(F32)
        out[q * part:(q + 1) * part, :] = total.astype(BF16)

    for d in range(2):
        for q in range(2):
            x_first(d, q).wait_send()
        w_first(d).wait_send()
        x_last(d).wait_send()
        for k in range(h):
            for q in range(2):
                if k < h - 1 or q == d:
                    p_copy(d, k, q).wait_send()
    w_last().wait_send()

    def drain(s, carry):
        for d in range(2):
            for q in range(2):
                x_copy(d, s, q).wait_send()
            w_copy(d, s).wait_send()
        return carry

    lax.fori_loop(2, h, drain, 0)

    def drain_sibling(s, carry):
        for d in range(2):
            b_copy(d, s).wait_send()
        z_copy(s).wait_send()
        return carry

    lax.fori_loop(0, h, drain_sibling, 0)


def ring_per_device(tokens, expert_ids, gate_fixed, gate_weight, up_weight, down_weight):
    n = lax.axis_size("expert")
    h = n // 2
    rows, half = tokens.shape
    ff = gate_weight.shape[2]
    dma = pltpu.SemaphoreType.DMA
    vmem = pl.BlockSpec(memory_space=pltpu.VMEM)
    hbm = pl.BlockSpec(memory_space=pl.ANY)
    return pl.pallas_call(
        functools.partial(ring_kernel, n),
        out_shape=jax.ShapeDtypeStruct((rows, half), BF16),
        in_specs=[vmem, vmem, vmem, hbm, hbm, hbm],
        out_specs=vmem,
        scratch_shapes=[
            pltpu.VMEM((h, 2, 2 * rows, half), BF16),
            pltpu.VMEM((h, 2, 8, 128), F32),
            pltpu.VMEM((2 * rows, ff), BF16),
            pltpu.VMEM((h, 2 * rows, half), F32),
            pltpu.VMEM((h, 2 * rows, half), BF16),
            pltpu.VMEM((h, 2 * rows, half), BF16),
            pltpu.VMEM((2, h, rows, half), BF16),
            pltpu.VMEM((2, h, rows, half), BF16),
            pltpu.VMEM((2 * half, ff), BF16),
            pltpu.VMEM((2 * half, ff), BF16),
            pltpu.VMEM((ff, 2 * half), BF16),
            dma((ff // min(TILE, ff),)), dma((ff // min(TILE, ff),)), dma((2 * half // DOWN_TILE,)),
            dma((2, h + 1, 2)), dma((2, h + 1, 2)),
            dma((2, h + 1)), dma((2, h + 1)),
            dma((2, h)), dma((2, h)),
            dma((h,)), dma((h,)),
            dma((2, h, 2)), dma((2, h, 2)),
        ],
        compiler_params=pltpu.CompilerParams(
            collective_id=0, has_side_effects=True, vmem_limit_bytes=60 * 1024 * 1024),
    )(tokens, expert_ids, gate_fixed, gate_weight, up_weight, down_weight)


CAP = 48
CHUNK = 16
PARTS = CAP // CHUNK
GU_TILE = 1024
ORDER = (1, 3, 2)


def slot_kernel(tok_in, ids_in, fixed_in, wg, wu, wd, out,
                tok, ids, fixed, small_sem, pk, xb, hid, yown, ysend, zin, psend, precv, rsend, ret, pick, vg, vu, vd,
                g_sem, u_sem, d_sem, z_ssem, z_rsem, y_ssem, y_rsem, b_ssem, b_rsem,
                k_ssem, k_rsem, p_ssem, p_rsem, r_ssem, r_rsem):
    rows, half = tok.shape
    ff = hid.shape[1]
    block = EXPERTS * CHUNK
    me = lax.axis_index("expert")
    core = lax.axis_index("tensor")
    other = 1 - core
    z, y = me // 2, me % 2

    def flip(r):
        hi = z // 2 if r < 2 else 1 - z // 2
        lo = z % 2 if r % 2 == 0 else 1 - z % 2
        return 2 * hi + lo

    sibling = {"tensor": other}
    across = {"expert": 2 * z + 1 - y}
    along = {r: {"expert": 2 * flip(r) + y} for r in range(1, EXPERTS)}

    barrier = pltpu.get_barrier_semaphore()
    for target in (*along.values(), across, sibling):
        pl.semaphore_signal(barrier, inc=1, device_id=target, device_id_type=pl.DeviceIdType.MESH)

    small = [pltpu.make_async_copy(src, dst, small_sem.at[i]) for i, (src, dst) in
             enumerate(((ids_in, ids), (tok_in, tok), (fixed_in, fixed)))]
    for copy in small:
        copy.start()

    tile = min(GU_TILE, ff)
    tiles = ff // tile

    def weight_copies(j):
        cols = pl.ds(j * tile, tile)
        return (pltpu.make_async_copy(wg.at[0, :, cols], vg.at[:, cols], g_sem.at[j]),
                pltpu.make_async_copy(wu.at[0, :, cols], vu.at[:, cols], u_sem.at[j]))

    def down_copy(which):
        cols = pl.ds(pl.multiple_of(which * half, half), half)
        return pltpu.make_async_copy(wd.at[0, :, cols], vd.at[:, cols], d_sem.at[which])

    for j in range(tiles):
        for copy in weight_copies(j):
            copy.start()
    down_copy(other).start()
    down_copy(core).start()

    small[0].wait()
    i0, i1 = ids[0:1, :], ids[1:2, :]
    match = [jnp.where((i0 == flip(r)) | (i1 == flip(r)), 1.0, 0.0) for r in range(EXPERTS)]
    before = (lax.broadcasted_iota(jnp.int32, (rows, rows), 0)
              < lax.broadcasted_iota(jnp.int32, (rows, rows), 1))
    stacked = jnp.concatenate(match + [jnp.zeros((8 - EXPERTS, rows), F32)], axis=0)
    pos = jnp.dot(stacked.astype(BF16), jnp.where(before, 1.0, 0.0).astype(BF16),
                  preferred_element_type=F32)
    slot = [jnp.where(match[r] > 0.0, pos[r:r + 1, :], -1.0) for r in range(EXPERTS)]
    number = lax.broadcasted_iota(jnp.int32, (CAP, rows), 0).astype(F32)
    small[1].wait()
    for r in range(EXPERTS):
        chosen = jnp.where(slot[r] == number, 1.0, 0.0).astype(BF16)
        pk[r] = jnp.dot(chosen, tok[...], preferred_element_type=F32).astype(BF16)
    pl.semaphore_wait(barrier, EXPERTS + 1)

    def remote(src, dst, ssem, rsem, target):
        return pltpu.make_async_remote_copy(
            src_ref=src, dst_ref=dst, send_sem=ssem, recv_sem=rsem,
            device_id=target, device_id_type=pl.DeviceIdType.MESH)

    def slots(c):
        return pl.ds(c * CHUNK, CHUNK)

    def unit(q, r):
        return pl.ds(q * block + r * CHUNK, CHUNK)

    def z_copy(r, c):
        return remote(pk.at[r, slots(c)], xb.at[c, core, unit(0, r)],
                      z_ssem.at[r, c], z_rsem.at[r, c], along[r])

    def y_copy(r, c):
        src = pk.at[0, slots(c)] if r == 0 else xb.at[c, core, unit(0, r)]
        return remote(src, xb.at[c, core, unit(1, r)], y_ssem.at[r, c], y_rsem.at[r, c], across)

    def b_copy(q, c):
        place = xb.at[c, core, pl.ds(q * block, block)]
        return remote(place, place, b_ssem.at[q, c], b_rsem.at[q, c], sibling)

    def k_copy(q, c):
        piece = pl.ds(q * block, block)
        return remote(ysend.at[c, piece], zin.at[c, piece], k_ssem.at[q, c], k_rsem.at[q, c], sibling)

    def p_copy(r, c):
        return remote(psend.at[c, unit(0, r)], precv.at[c, unit(0, r)],
                      p_ssem.at[r, c], p_rsem.at[r, c], across)

    def r_copy(r, c):
        dst = ret.at[pl.ds(r * CAP + c * CHUNK, CHUNK)]
        return remote(rsend.at[c, unit(0, r)], dst, r_ssem.at[r, c], r_rsem.at[r, c], along[r])

    for c in range(PARTS):
        for r in ORDER:
            z_copy(r, c).start()
        y_copy(0, c).start()

    for c in range(PARTS):
        xb[c, core, 0:CHUNK, :] = pk[0, c * CHUNK:(c + 1) * CHUNK, :]

    small[2].wait()
    f0, f1 = fixed[0:1, :].astype(F32), fixed[1:2, :].astype(F32)
    s0, s1 = f0 / (f0 + f1), f1 / (f0 + f1)
    diag = (lax.broadcasted_iota(jnp.int32, (rows, rows), 0)
            == lax.broadcasted_iota(jnp.int32, (rows, rows), 1))

    def column(row):
        return jnp.sum(jnp.where(diag, row, 0.0), axis=1, keepdims=True)

    lane = lax.broadcasted_iota(jnp.int32, (rows, EXPERTS * CAP), 1).astype(F32)
    weigh = jnp.zeros((rows, EXPERTS * CAP), F32)
    for r in range(EXPERTS):
        e = flip(r)
        share = jnp.where(i0 == e, s0, 0.0) + jnp.where(i1 == e, s1, 0.0)
        place = column(jnp.where(match[r] > 0.0, pos[r:r + 1, :] + float(r * CAP), -1.0))
        weigh = weigh + jnp.where(place == lane, column(share), 0.0)
    high = weigh.astype(BF16)
    pick[0:rows, :] = high
    pick[rows:2 * rows, :] = (weigh - high.astype(F32)).astype(BF16)

    def relay(c):
        for r in ORDER:
            z_copy(r, c).wait_recv()
            y_copy(r, c).start()
        b_copy(0, c).start()

    def spread(c):
        for r in range(EXPERTS):
            y_copy(r, c).wait_recv()
        b_copy(1, c).start()

    def to_partner(c):
        k_copy(1, c).wait_recv()
        for r in (3, 2, 1, 0):
            piece = pl.ds(block + r * CHUNK, CHUNK)
            psend[c, unit(0, r), :] = (yown[c, piece, :] + zin[c, piece, :].astype(F32)).astype(BF16)
            p_copy(r, c).start()

    def to_origin(c, r):
        if r == 3:
            k_copy(0, c).wait_recv()
        p_copy(r, c).wait_recv()
        piece = unit(0, r)
        total = (yown[c, piece, :] + zin[c, piece, :].astype(F32)
                 + precv[c, piece, :].astype(F32)).astype(BF16)
        if r == 0:
            ret[slots(c), :] = total
        else:
            rsend[c, piece, :] = total
            r_copy(r, c).start()

    relay(0)
    spread(0)
    relay(1)

    def down(c, which):
        if c == 0:
            down_copy(which).wait()
        cols = pl.ds(pl.multiple_of(which * half, half), half)
        return jnp.dot(hid[...], vd[:, cols], preferred_element_type=F32)

    for c in range(PARTS):
        if c > 0:
            to_partner(c - 1)
        b_copy(0, c).wait_recv()
        b_copy(1, c).wait_recv()
        if c > 1:
            to_origin(c - 2, 2)
        for j in range(tiles):
            if c == 0:
                for copy in weight_copies(j):
                    copy.wait()
            cols = pl.ds(j * tile, tile)
            a, b = xb[c, 0], xb[c, 1]
            g = (jnp.dot(a, vg[0:half, cols], preferred_element_type=F32)
                 + jnp.dot(b, vg[half:2 * half, cols], preferred_element_type=F32))
            u = (jnp.dot(a, vu[0:half, cols], preferred_element_type=F32)
                 + jnp.dot(b, vu[half:2 * half, cols], preferred_element_type=F32))
            hid[:, cols] = (g / (1.0 + jnp.exp(-g)) * u).astype(BF16)
            if j == 0 and c > 1:
                to_origin(c - 2, 1)
                to_origin(c - 2, 0)
        if c < PARTS - 2:
            relay(c + 2)
        ysend[c] = down(c, other).astype(BF16)
        k_copy(1, c).start()
        k_copy(0, c).start()
        if c < PARTS - 1:
            spread(c + 1)
        if c > 0:
            to_origin(c - 1, 3)
        yown[c] = down(c, core)

    to_origin(PARTS - 2, 2)
    to_partner(PARTS - 1)
    for r in (1, 0):
        to_origin(PARTS - 2, r)
    for c in range(PARTS):
        for r in range(EXPERTS):
            if r:
                z_copy(r, c).wait_send()
            y_copy(r, c).wait_send()
        for q in range(2):
            b_copy(q, c).wait_send()
        for q in range(2):
            k_copy(q, c).wait_send()
    for r in (3, 2, 1, 0):
        to_origin(PARTS - 1, r)
    for c in range(PARTS):
        for r in range(EXPERTS):
            p_copy(r, c).wait_send()
            if r:
                r_copy(r, c).wait_send()

    for c in range(PARTS):
        for r in (1, 2, 3):
            r_copy(r, c).wait_recv()
    mixed = jnp.dot(pick[...], ret[...], preferred_element_type=F32)
    out[...] = (mixed[0:rows] + mixed[rows:2 * rows]).astype(BF16)


def slot_per_device(tokens, expert_ids, gate_fixed, gate_weight, up_weight, down_weight):
    rows, half = tokens.shape
    ff = gate_weight.shape[2]
    tiles = ff // min(GU_TILE, ff)
    many = 2 * EXPERTS * CHUNK
    dma = pltpu.SemaphoreType.DMA
    vmem = pl.BlockSpec(memory_space=pltpu.VMEM)
    hbm = pl.BlockSpec(memory_space=pl.ANY)
    return pl.pallas_call(
        slot_kernel,
        out_shape=pltpu.VMEM((rows, half), BF16),
        in_specs=[hbm] * 6,
        out_specs=vmem,
        scratch_shapes=[
            pltpu.VMEM((rows, half), BF16),
            pltpu.VMEM((2, rows), jnp.int32),
            pltpu.VMEM((2, rows), jnp.int32),
            dma((3,)),
            pltpu.VMEM((EXPERTS, CAP, half), BF16),
            pltpu.VMEM((PARTS, 2, many, half), BF16),
            pltpu.VMEM((many, ff), BF16),
            pltpu.VMEM((PARTS, many, half), F32),
            pltpu.VMEM((PARTS, many, half), BF16),
            pltpu.VMEM((PARTS, many, half), BF16),
            pltpu.VMEM((PARTS, many // 2, half), BF16),
            pltpu.VMEM((PARTS, many // 2, half), BF16),
            pltpu.VMEM((PARTS, many // 2, half), BF16),
            pltpu.VMEM((EXPERTS * CAP, half), BF16),
            pltpu.VMEM((2 * rows, EXPERTS * CAP), BF16),
            pltpu.VMEM((2 * half, ff), BF16),
            pltpu.VMEM((2 * half, ff), BF16),
            pltpu.VMEM((ff, 2 * half), BF16),
            dma((tiles,)), dma((tiles,)), dma((2,)),
            dma((EXPERTS, PARTS)), dma((EXPERTS, PARTS)),
            dma((EXPERTS, PARTS)), dma((EXPERTS, PARTS)),
            dma((2, PARTS)), dma((2, PARTS)),
            dma((2, PARTS)), dma((2, PARTS)),
            dma((EXPERTS, PARTS)), dma((EXPERTS, PARTS)),
            dma((EXPERTS, PARTS)), dma((EXPERTS, PARTS)),
        ],
        compiler_params=pltpu.CompilerParams(
            collective_id=0, has_side_effects=True, vmem_limit_bytes=60 * 1024 * 1024),
    )(tokens, expert_ids.T, gate_fixed.T, gate_weight, up_weight, down_weight)


def solution(mesh):
    placed = (
        P(("group", "expert"), "tensor"),
        P(("group", "expert"), None),
        P(("group", "expert"), None),
        P("expert", None, "tensor"),
        P("expert", None, "tensor"),
        P("expert", "tensor", None),
    )
    return jax.shard_map(
        slot_per_device if mesh.shape["expert"] == 2 * EXPERTS else ring_per_device,
        mesh=mesh,
        in_specs=placed,
        out_specs=P(("group", "expert"), "tensor"),
        check_vma=False,
    )
```

```python
import functools

import jax
import jax.numpy as jnp
from jax import lax
from jax.experimental import pallas as pl
from jax.experimental.pallas import tpu as pltpu
from jax.sharding import PartitionSpec as P

EXPERTS = 4
TILE = 1024
DOWN_TILE = 768
F32 = jnp.float32
BF16 = jnp.bfloat16


def ring_kernel(n, tok, ids, fixed, wg, wu, wd, out,
           xb, wt, hid, yown, ysend, zin, psend, precv, vg, vu, vd,
           g_sem, u_sem, d_sem, x_ssem, x_rsem, w_ssem, w_rsem, b_ssem, b_rsem,
           z_ssem, z_rsem, p_ssem, p_rsem):
    h = n // 2
    rows, half = tok.shape
    part = rows // 2
    me = lax.axis_index("expert")
    core = lax.axis_index("tensor")
    other = 1 - core
    expert = me // (n // EXPERTS)
    odd = me % 2
    pos = (1 - odd) * (me // 2) + odd * (n - 1 - me // 2)

    def at_pos(p):
        p = (p + n) % n
        back = p // h
        return (1 - back) * (2 * p) + back * (2 * (n - 1 - p) + 1)

    onward = ({"expert": at_pos(pos + 1)}, {"expert": at_pos(pos - 1)})
    sibling = {"tensor": other}

    ff = hid.shape[1]
    tile = min(TILE, ff)
    j_hidden = ff // tile
    j_half = half // DOWN_TILE

    def hidden_cols(j):
        return pl.ds(pl.multiple_of(j * tile, tile), tile)

    def out_cols(j):
        return pl.ds(pl.multiple_of(j * DOWN_TILE, DOWN_TILE), DOWN_TILE)

    def weight_copies(j):
        cols = hidden_cols(j)
        return (pltpu.make_async_copy(wg.at[0, :, cols], vg.at[:, cols], g_sem.at[j]),
                pltpu.make_async_copy(wu.at[0, :, cols], vu.at[:, cols], u_sem.at[j]))

    def down_copy(j):
        cols = out_cols(j)
        return pltpu.make_async_copy(wd.at[0, :, cols], vd.at[:, cols], d_sem.at[j])

    @pl.loop(0, j_hidden)
    def _(j):
        for copy in weight_copies(j):
            copy.start()

    @pl.loop(0, 2 * j_half)
    def _(j):
        down_copy(j).start()

    barrier = pltpu.get_barrier_semaphore()
    for target in onward + (sibling,):
        pl.semaphore_signal(barrier, inc=1, device_id=target, device_id_type=pl.DeviceIdType.MESH)

    diag = (lax.broadcasted_iota(jnp.int32, (rows, 128), 0)
            == lax.broadcasted_iota(jnp.int32, (rows, 128), 1))
    f0 = fixed[:, 0:1].astype(F32)
    f1 = fixed[:, 1:2].astype(F32)
    total = f0 + f1
    s0, s1 = f0 / total, f1 / total
    i0, i1 = ids[:, 0:1], ids[:, 1:2]
    wt[0, 0] = jnp.zeros((8, 128), F32)
    for e in range(EXPERTS):
        col = jnp.where(i0 == e, s0, 0.0) + jnp.where(i1 == e, s1, 0.0)
        wt[0, 0, e:e + 1, :] = jnp.sum(jnp.where(diag, col, 0.0), axis=0, keepdims=True)
    xb[0, core, 0:rows, :] = tok[...]
    pl.semaphore_wait(barrier, 3)

    def remote(src, dst, ssem, rsem, target):
        return pltpu.make_async_remote_copy(
            src_ref=src, dst_ref=dst, send_sem=ssem, recv_sem=rsem,
            device_id=target, device_id_type=pl.DeviceIdType.MESH)

    def x_copy(d, s, q):
        piece = pl.ds(d * rows + q * part, part)
        return remote(xb.at[s - 1, core, piece], xb.at[s, core, piece],
                      x_ssem.at[d, s, q], x_rsem.at[d, s, q], onward[d])

    def x_first(d, q):
        return remote(xb.at[0, core, pl.ds(q * part, part)],
                      xb.at[1, core, pl.ds(d * rows + q * part, part)],
                      x_ssem.at[d, 1, q], x_rsem.at[d, 1, q], onward[d])

    def x_last(d):
        return remote(xb.at[h - 1, core, pl.ds(d * rows + d * part, part)],
                      xb.at[0, core, pl.ds(rows + d * part, part)],
                      x_ssem.at[d, h, d], x_rsem.at[d, h, d], onward[d])

    def w_copy(d, s):
        return remote(wt.at[s - 1, d], wt.at[s, d], w_ssem.at[d, s], w_rsem.at[d, s], onward[d])

    def w_first(d):
        return remote(wt.at[0, 0], wt.at[1, d], w_ssem.at[d, 1], w_rsem.at[d, 1], onward[d])

    def w_last():
        return remote(wt.at[h - 1, 0], wt.at[0, 1], w_ssem.at[0, h], w_rsem.at[0, h], onward[0])

    def b_copy(d, s):
        place = xb.at[s, core, pl.ds(d * rows, rows)]
        return remote(place, place, b_ssem.at[d, s], b_rsem.at[d, s], sibling)

    def z_copy(s):
        return remote(ysend.at[s], zin.at[s], z_ssem.at[s], z_rsem.at[s], sibling)

    for d in range(2):
        w_first(d).start()
    for q in range(2):
        for d in range(2):
            x_first(d, d if q == 0 else 1 - d).start()
    b_copy(0, 0).start()

    def compute(s, first):
        @pl.loop(0, j_hidden)
        def _(j):
            cols = hidden_cols(j)

            @pl.when(first)
            def _():
                for copy in weight_copies(j):
                    copy.wait()

            a, b = xb[s, 0], xb[s, 1]
            g = (jnp.dot(a, vg[0:half, cols], preferred_element_type=F32)
                 + jnp.dot(b, vg[half:2 * half, cols], preferred_element_type=F32))
            u = (jnp.dot(a, vu[0:half, cols], preferred_element_type=F32)
                 + jnp.dot(b, vu[half:2 * half, cols], preferred_element_type=F32))
            hid[:, cols] = (g / (1.0 + jnp.exp(-g)) * u).astype(BF16)

        share = jnp.concatenate(
            [jnp.sum(jnp.where(diag, wt[s, d, pl.ds(expert, 1), :], 0.0), axis=1, keepdims=True)
             for d in range(2)], axis=0)

        def down(j, which):
            cols = pl.ds(pl.multiple_of(which * half + j * DOWN_TILE, DOWN_TILE), DOWN_TILE)

            @pl.when(first)
            def _():
                down_copy(which * j_half + j).wait()

            return jnp.dot(hid[...], vd[:, cols], preferred_element_type=F32) * share

        @pl.loop(0, j_half)
        def _(j):
            ysend[s, :, out_cols(j)] = down(j, other).astype(BF16)

        z_copy(s).start()

        @pl.loop(0, j_half)
        def _(j):
            yown[s, :, out_cols(j)] = down(j, core)

    def step(s, carry):
        for turn in range(2):
            for d in range(2):
                q = d if turn == 0 else 1 - d
                x_copy(d, s, q).wait_recv()

                @pl.when(s < h - 1)
                def _():
                    x_copy(d, s + 1, q).start()

                if turn == 0:
                    @pl.when(s == h - 1)
                    def _():
                        x_last(d).start()

        for d in range(2):
            w_copy(d, s).wait_recv()

        @pl.when(s < h - 1)
        def _():
            for d in range(2):
                w_copy(d, s + 1).start()

        @pl.when(s == h - 1)
        def _():
            w_last().start()

        for d in range(2):
            b_copy(d, s).start()
        for d in range(2):
            b_copy(d, s).wait_recv()
        compute(s, s == 1)
        return carry

    lax.fori_loop(1, h, step, 0)
    for d in range(2):
        x_last(d).wait_recv()
    w_last().wait_recv()
    b_copy(1, 0).start()
    b_copy(0, 0).wait_recv()
    b_copy(1, 0).wait_recv()
    compute(0, False)

    def p_copy(d, k, q):
        piece = pl.ds(q * part, part)
        return remote(psend.at[d, k, piece], precv.at[d, k, piece],
                      p_ssem.at[d, k, q], p_rsem.at[d, k, q], onward[d])

    z_copy(0).wait_recv()
    for k in range(h, 0, -1):
        slot = k % h
        if k < h:
            z_copy(k).wait_recv()
        for turn in range(2):
            for d in range(2):
                q = (1 - d) if turn == 0 else d
                if k == h and q != d:
                    continue
                base = (rows if k == h or d == 0 else 0) + q * part
                total = yown[slot, base:base + part, :] + zin[slot, base:base + part, :].astype(F32)
                if k < h - 1 or (k == h - 1 and q == d):
                    p_copy(d, k, q).wait_recv()
                    total = total + precv[d, k, q * part:(q + 1) * part, :].astype(F32)
                psend[d, k - 1, q * part:(q + 1) * part, :] = total.astype(BF16)
                p_copy(d, k - 1, q).start()
    for q in (0, 1):
        total = yown[0, q * part:(q + 1) * part, :] + zin[0, q * part:(q + 1) * part, :].astype(F32)
        for d in range(2):
            p_copy(d, 0, q).wait_recv()
            total = total + precv[d, 0, q * part:(q + 1) * part, :].astype(F32)
        out[q * part:(q + 1) * part, :] = total.astype(BF16)

    for d in range(2):
        for q in range(2):
            x_first(d, q).wait_send()
        w_first(d).wait_send()
        x_last(d).wait_send()
        for k in range(h):
            for q in range(2):
                if k < h - 1 or q == d:
                    p_copy(d, k, q).wait_send()
    w_last().wait_send()

    def drain(s, carry):
        for d in range(2):
            for q in range(2):
                x_copy(d, s, q).wait_send()
            w_copy(d, s).wait_send()
        return carry

    lax.fori_loop(2, h, drain, 0)

    def drain_sibling(s, carry):
        for d in range(2):
            b_copy(d, s).wait_send()
        z_copy(s).wait_send()
        return carry

    lax.fori_loop(0, h, drain_sibling, 0)


def ring_per_device(tokens, expert_ids, gate_fixed, gate_weight, up_weight, down_weight):
    n = lax.axis_size("expert")
    h = n // 2
    rows, half = tokens.shape
    ff = gate_weight.shape[2]
    dma = pltpu.SemaphoreType.DMA
    vmem = pl.BlockSpec(memory_space=pltpu.VMEM)
    hbm = pl.BlockSpec(memory_space=pl.ANY)
    return pl.pallas_call(
        functools.partial(ring_kernel, n),
        out_shape=jax.ShapeDtypeStruct((rows, half), BF16),
        in_specs=[vmem, vmem, vmem, hbm, hbm, hbm],
        out_specs=vmem,
        scratch_shapes=[
            pltpu.VMEM((h, 2, 2 * rows, half), BF16),
            pltpu.VMEM((h, 2, 8, 128), F32),
            pltpu.VMEM((2 * rows, ff), BF16),
            pltpu.VMEM((h, 2 * rows, half), F32),
            pltpu.VMEM((h, 2 * rows, half), BF16),
            pltpu.VMEM((h, 2 * rows, half), BF16),
            pltpu.VMEM((2, h, rows, half), BF16),
            pltpu.VMEM((2, h, rows, half), BF16),
            pltpu.VMEM((2 * half, ff), BF16),
            pltpu.VMEM((2 * half, ff), BF16),
            pltpu.VMEM((ff, 2 * half), BF16),
            dma((ff // min(TILE, ff),)), dma((ff // min(TILE, ff),)), dma((2 * half // DOWN_TILE,)),
            dma((2, h + 1, 2)), dma((2, h + 1, 2)),
            dma((2, h + 1)), dma((2, h + 1)),
            dma((2, h)), dma((2, h)),
            dma((h,)), dma((h,)),
            dma((2, h, 2)), dma((2, h, 2)),
        ],
        compiler_params=pltpu.CompilerParams(
            collective_id=0, has_side_effects=True, vmem_limit_bytes=60 * 1024 * 1024),
    )(tokens, expert_ids, gate_fixed, gate_weight, up_weight, down_weight)


CAP = 48
CHUNK = 16
PARTS = CAP // CHUNK
GU_TILE = 1024
ORDER = (1, 3, 2)


def slot_kernel(tok_in, ids_in, fixed_in, wg, wu, wd, out,
                tok, ids, fixed, small_sem, pk, xb, hid, yown, ysend, zin, psend, precv, rsend, ret, pick, vg, vu, vd,
                g_sem, u_sem, d_sem, z_ssem, z_rsem, y_ssem, y_rsem, b_ssem, b_rsem,
                k_ssem, k_rsem, p_ssem, p_rsem, r_ssem, r_rsem):
    rows, half = tok.shape
    ff = hid.shape[1]
    block = EXPERTS * CHUNK
    me = lax.axis_index("expert")
    core = lax.axis_index("tensor")
    other = 1 - core
    z, y = me // 2, me % 2

    def flip(r):
        hi = z // 2 if r < 2 else 1 - z // 2
        lo = z % 2 if r % 2 == 0 else 1 - z % 2
        return 2 * hi + lo

    sibling = {"tensor": other}
    across = {"expert": 2 * z + 1 - y}
    along = {r: {"expert": 2 * flip(r) + y} for r in range(1, EXPERTS)}

    barrier = pltpu.get_barrier_semaphore()
    for target in (*along.values(), across, sibling):
        pl.semaphore_signal(barrier, inc=1, device_id=target, device_id_type=pl.DeviceIdType.MESH)

    small = [pltpu.make_async_copy(src, dst, small_sem.at[i]) for i, (src, dst) in
             enumerate(((ids_in, ids), (tok_in, tok), (fixed_in, fixed)))]
    for copy in small:
        copy.start()

    tile = min(GU_TILE, ff)
    tiles = ff // tile

    def weight_copies(j):
        cols = pl.ds(j * tile, tile)
        return (pltpu.make_async_copy(wg.at[0, :, cols], vg.at[:, cols], g_sem.at[j]),
                pltpu.make_async_copy(wu.at[0, :, cols], vu.at[:, cols], u_sem.at[j]))

    def down_copy(which):
        cols = pl.ds(pl.multiple_of(which * half, half), half)
        return pltpu.make_async_copy(wd.at[0, :, cols], vd.at[:, cols], d_sem.at[which])

    for j in range(tiles):
        for copy in weight_copies(j):
            copy.start()
    down_copy(other).start()
    down_copy(core).start()

    small[0].wait()
    i0, i1 = ids[0:1, :], ids[1:2, :]
    match = [jnp.where((i0 == flip(r)) | (i1 == flip(r)), 1.0, 0.0) for r in range(EXPERTS)]
    before = (lax.broadcasted_iota(jnp.int32, (rows, rows), 0)
              < lax.broadcasted_iota(jnp.int32, (rows, rows), 1))
    stacked = jnp.concatenate(match + [jnp.zeros((8 - EXPERTS, rows), F32)], axis=0)
    pos = jnp.dot(stacked.astype(BF16), jnp.where(before, 1.0, 0.0).astype(BF16),
                  preferred_element_type=F32)
    slot = [jnp.where(match[r] > 0.0, pos[r:r + 1, :], -1.0) for r in range(EXPERTS)]
    number = lax.broadcasted_iota(jnp.int32, (CAP, rows), 0).astype(F32)
    small[1].wait()
    for r in range(EXPERTS):
        chosen = jnp.where(slot[r] == number, 1.0, 0.0).astype(BF16)
        pk[r] = jnp.dot(chosen, tok[...], preferred_element_type=F32).astype(BF16)
    pl.semaphore_wait(barrier, EXPERTS + 1)

    def remote(src, dst, ssem, rsem, target):
        return pltpu.make_async_remote_copy(
            src_ref=src, dst_ref=dst, send_sem=ssem, recv_sem=rsem,
            device_id=target, device_id_type=pl.DeviceIdType.MESH)

    def slots(c):
        return pl.ds(c * CHUNK, CHUNK)

    def unit(q, r):
        return pl.ds(q * block + r * CHUNK, CHUNK)

    def z_copy(r, c):
        return remote(pk.at[r, slots(c)], xb.at[c, core, unit(0, r)],
                      z_ssem.at[r, c], z_rsem.at[r, c], along[r])

    def y_copy(r, c):
        src = pk.at[0, slots(c)] if r == 0 else xb.at[c, core, unit(0, r)]
        return remote(src, xb.at[c, core, unit(1, r)], y_ssem.at[r, c], y_rsem.at[r, c], across)

    def b_copy(q, c):
        place = xb.at[c, core, pl.ds(q * block, block)]
        return remote(place, place, b_ssem.at[q, c], b_rsem.at[q, c], sibling)

    def k_copy(q, c):
        piece = pl.ds(q * block, block)
        return remote(ysend.at[c, piece], zin.at[c, piece], k_ssem.at[q, c], k_rsem.at[q, c], sibling)

    def p_copy(r, c):
        return remote(psend.at[c, unit(0, r)], precv.at[c, unit(0, r)],
                      p_ssem.at[r, c], p_rsem.at[r, c], across)

    def r_copy(r, c):
        dst = ret.at[pl.ds(r * CAP + c * CHUNK, CHUNK)]
        return remote(rsend.at[c, unit(0, r)], dst, r_ssem.at[r, c], r_rsem.at[r, c], along[r])

    for c in range(PARTS):
        for r in ORDER:
            z_copy(r, c).start()
        y_copy(0, c).start()

    for c in range(PARTS):
        xb[c, core, 0:CHUNK, :] = pk[0, c * CHUNK:(c + 1) * CHUNK, :]

    small[2].wait()
    f0, f1 = fixed[0:1, :].astype(F32), fixed[1:2, :].astype(F32)
    s0, s1 = f0 / (f0 + f1), f1 / (f0 + f1)
    diag = (lax.broadcasted_iota(jnp.int32, (rows, rows), 0)
            == lax.broadcasted_iota(jnp.int32, (rows, rows), 1))

    def column(row):
        return jnp.sum(jnp.where(diag, row, 0.0), axis=1, keepdims=True)

    lane = lax.broadcasted_iota(jnp.int32, (rows, EXPERTS * CAP), 1).astype(F32)
    weigh = jnp.zeros((rows, EXPERTS * CAP), F32)
    for r in range(EXPERTS):
        e = flip(r)
        share = jnp.where(i0 == e, s0, 0.0) + jnp.where(i1 == e, s1, 0.0)
        place = column(jnp.where(match[r] > 0.0, pos[r:r + 1, :] + float(r * CAP), -1.0))
        weigh = weigh + jnp.where(place == lane, column(share), 0.0)
    high = weigh.astype(BF16)
    pick[0:rows, :] = high
    pick[rows:2 * rows, :] = (weigh - high.astype(F32)).astype(BF16)

    def relay(c):
        for r in ORDER:
            z_copy(r, c).wait_recv()
            y_copy(r, c).start()
        b_copy(0, c).start()

    def spread(c):
        for r in range(EXPERTS):
            y_copy(r, c).wait_recv()
        b_copy(1, c).start()

    def to_partner(c):
        k_copy(1, c).wait_recv()
        for r in (3, 2, 1, 0):
            piece = pl.ds(block + r * CHUNK, CHUNK)
            psend[c, unit(0, r), :] = (yown[c, piece, :] + zin[c, piece, :].astype(F32)).astype(BF16)
            p_copy(r, c).start()

    def to_origin(c, r):
        if r == 3:
            k_copy(0, c).wait_recv()
        p_copy(r, c).wait_recv()
        piece = unit(0, r)
        total = (yown[c, piece, :] + zin[c, piece, :].astype(F32)
                 + precv[c, piece, :].astype(F32)).astype(BF16)
        if r == 0:
            ret[slots(c), :] = total
        else:
            rsend[c, piece, :] = total
            r_copy(r, c).start()

    relay(0)
    spread(0)
    relay(1)

    def down(c, which):
        if c == 0:
            down_copy(which).wait()
        cols = pl.ds(pl.multiple_of(which * half, half), half)
        return jnp.dot(hid[...], vd[:, cols], preferred_element_type=F32)

    for c in range(PARTS):
        if c > 0:
            to_partner(c - 1)
        b_copy(0, c).wait_recv()
        b_copy(1, c).wait_recv()
        if c > 1:
            to_origin(c - 2, 2)
        for j in range(tiles):
            if c == 0:
                for copy in weight_copies(j):
                    copy.wait()
            cols = pl.ds(j * tile, tile)
            a, b = xb[c, 0], xb[c, 1]
            g = (jnp.dot(a, vg[0:half, cols], preferred_element_type=F32)
                 + jnp.dot(b, vg[half:2 * half, cols], preferred_element_type=F32))
            u = (jnp.dot(a, vu[0:half, cols], preferred_element_type=F32)
                 + jnp.dot(b, vu[half:2 * half, cols], preferred_element_type=F32))
            hid[:, cols] = (g / (1.0 + jnp.exp(-g)) * u).astype(BF16)
            if j == 0 and c > 1:
                to_origin(c - 2, 1)
                to_origin(c - 2, 0)
        if c < PARTS - 2:
            relay(c + 2)
        ysend[c] = down(c, other).astype(BF16)
        k_copy(1, c).start()
        k_copy(0, c).start()
        if c < PARTS - 1:
            spread(c + 1)
        if c > 0:
            to_origin(c - 1, 3)
        yown[c] = down(c, core)

    to_partner(PARTS - 1)
    to_origin(PARTS - 2, 2)
    for r in (1, 0):
        to_origin(PARTS - 2, r)
    for c in range(PARTS):
        for r in range(EXPERTS):
            if r:
                z_copy(r, c).wait_send()
            y_copy(r, c).wait_send()
        for q in range(2):
            b_copy(q, c).wait_send()
        for q in range(2):
            k_copy(q, c).wait_send()
    for r in (3, 2, 1, 0):
        to_origin(PARTS - 1, r)
    for c in range(PARTS):
        for r in range(EXPERTS):
            p_copy(r, c).wait_send()
            if r:
                r_copy(r, c).wait_send()

    for c in range(PARTS):
        for r in (1, 2, 3):
            r_copy(r, c).wait_recv()
    mixed = jnp.dot(pick[...], ret[...], preferred_element_type=F32)
    out[...] = (mixed[0:rows] + mixed[rows:2 * rows]).astype(BF16)


def slot_per_device(tokens, expert_ids, gate_fixed, gate_weight, up_weight, down_weight):
    rows, half = tokens.shape
    ff = gate_weight.shape[2]
    tiles = ff // min(GU_TILE, ff)
    many = 2 * EXPERTS * CHUNK
    dma = pltpu.SemaphoreType.DMA
    vmem = pl.BlockSpec(memory_space=pltpu.VMEM)
    hbm = pl.BlockSpec(memory_space=pl.ANY)
    return pl.pallas_call(
        slot_kernel,
        out_shape=pltpu.VMEM((rows, half), BF16),
        in_specs=[hbm] * 6,
        out_specs=vmem,
        scratch_shapes=[
            pltpu.VMEM((rows, half), BF16),
            pltpu.VMEM((2, rows), jnp.int32),
            pltpu.VMEM((2, rows), jnp.int32),
            dma((3,)),
            pltpu.VMEM((EXPERTS, CAP, half), BF16),
            pltpu.VMEM((PARTS, 2, many, half), BF16),
            pltpu.VMEM((many, ff), BF16),
            pltpu.VMEM((PARTS, many, half), F32),
            pltpu.VMEM((PARTS, many, half), BF16),
            pltpu.VMEM((PARTS, many, half), BF16),
            pltpu.VMEM((PARTS, many // 2, half), BF16),
            pltpu.VMEM((PARTS, many // 2, half), BF16),
            pltpu.VMEM((PARTS, many // 2, half), BF16),
            pltpu.VMEM((EXPERTS * CAP, half), BF16),
            pltpu.VMEM((2 * rows, EXPERTS * CAP), BF16),
            pltpu.VMEM((2 * half, ff), BF16),
            pltpu.VMEM((2 * half, ff), BF16),
            pltpu.VMEM((ff, 2 * half), BF16),
            dma((tiles,)), dma((tiles,)), dma((2,)),
            dma((EXPERTS, PARTS)), dma((EXPERTS, PARTS)),
            dma((EXPERTS, PARTS)), dma((EXPERTS, PARTS)),
            dma((2, PARTS)), dma((2, PARTS)),
            dma((2, PARTS)), dma((2, PARTS)),
            dma((EXPERTS, PARTS)), dma((EXPERTS, PARTS)),
            dma((EXPERTS, PARTS)), dma((EXPERTS, PARTS)),
        ],
        compiler_params=pltpu.CompilerParams(
            collective_id=0, has_side_effects=True, vmem_limit_bytes=60 * 1024 * 1024),
    )(tokens, expert_ids.T, gate_fixed.T, gate_weight, up_weight, down_weight)


def solution(mesh):
    placed = (
        P(("group", "expert"), "tensor"),
        P(("group", "expert"), None),
        P(("group", "expert"), None),
        P("expert", None, "tensor"),
        P("expert", None, "tensor"),
        P("expert", "tensor", None),
    )
    return jax.shard_map(
        slot_per_device if mesh.shape["expert"] == 2 * EXPERTS else ring_per_device,
        mesh=mesh,
        in_specs=placed,
        out_specs=P(("group", "expert"), "tensor"),
        check_vma=False,
    )
```
